32 devices in a mesh: groups: 2 (over x), owner: 8 (over z, y), slab: 2 (over core).
Axes of the slice: x: 2, y: 2, z: 4, core: 2. Of those that a mesh axis runs over, the one named last changes fastest.
Arguments:
- queries: bfloat16 [16, 4, 112, 2560], P(('groups', 'owner'), 'slab'), parts along dimension 0, may hold values from -40 to 40
- key_value: bfloat16 [2, 16, 4, 112, 2560], P(None, ('groups', 'owner'), 'slab'), parts along dimension 1, may hold values from -8 to 8
- keep: int32 [8], P('groups'), parts along dimension 0, may hold values 0 or 1
- windows: int32 [8, 3], P('groups'), parts along dimension 0, may hold values from 0 to 7, as said below
- gate: float32 [8, 5120], P('groups'), parts along dimension 0, may hold values from -1.5 to 1.5
- out_weight: bfloat16 [2560, 5120], P('owner'), may hold values from -0.125 to 0.125
Outputs:
- output: bfloat16 [16, 4, 112, 5120], P(('groups', 'owner'), 'slab'), parts along dimension 0
The draws below stay inside these ranges and needn't reach their ends.
There are 2 independent parts, one for each index of `groups`. The reference program is written for one: setup_inputs(seed, part) draws one part's arguments, and reference() takes and returns one part's arrays. A program takes and returns all parts, laid end to end along the dimension named above; an argument that names none is the same for every part. Nothing has to cross between parts.
Inputs may be any that keep to these rules, and one draw needn't show every extreme that they name: `windows`: column 0 runs from 0 to 1, column 1 from 1 to 4, column 2 from 1 to 7; the first request takes the largest value of each column.
All inputs are finite; a program needn't handle non-finite values.
Results may differ from the reference program's by a relative error of at most 0.0057.
Values may be sent and summed in bfloat16 or wider, within the bound.
A program may use at most 128 MiB of HBM per device.

```python
import math
import jax
import jax.numpy as jnp
from jax import lax

D = 5120
HEADS = 20
HEAD_DIM = 128
HH = 2560
HB = 8
WB = 14
HALO = 1
SP = 112
FRAMES = 4
STREAMS = 8
REQUESTS = 4


def key_base(key):
    shape = (STREAMS, FRAMES, SP, HH)
    base_key = jax.random.fold_in(key, 11)
    raw = jnp.clip(jax.random.normal(base_key, shape, jnp.float32), -6.0, 6.0)
    return raw


def draw_key_value(key, part):
    shape = (STREAMS, FRAMES, SP, HH)
    raw = key_base(key)
    keys = raw
    values = jnp.clip(jax.random.normal(jax.random.fold_in(key, 13), shape, jnp.float32), -6.0, 6.0)
    return jnp.stack([keys, values], axis=0).astype(jnp.bfloat16)


def draw_queries(key, part):
    shape = (STREAMS, FRAMES, SP, HH)
    result = jnp.clip(jax.random.normal(jax.random.fold_in(key, 14), shape, jnp.float32), -6.0, 6.0)
    return result.astype(jnp.bfloat16)


def draw_windows(key, part):
    depth = jax.random.randint(jax.random.fold_in(key, 21), (REQUESTS,), 0, HALO + 1)
    height = jax.random.randint(jax.random.fold_in(key, 22), (REQUESTS,), 1, HB // 2 + 1)
    breadth = jax.random.randint(jax.random.fold_in(key, 23), (REQUESTS,), 1, WB // 2 + 1)
    leading = jnp.arange(REQUESTS, dtype=jnp.int32) == 0
    depth = jnp.where(leading, HALO, depth)
    height = jnp.where(leading, HB // 2, height)
    breadth = jnp.where(leading, WB // 2, breadth)
    return jnp.stack([depth, height, breadth], axis=1).astype(jnp.int32)


def set_ends(entries, rng, smallest, top_value):
    longest = entries.shape.index(max(entries.shape))
    spots = []
    for shift in (0, 1):
        where = [jax.random.randint(jax.random.fold_in(rng, axis), (), 0, length) for axis, length in enumerate(entries.shape)]
        where[longest] = (where[longest] + shift) % entries.shape[longest]
        spots.append(tuple(where))
    return entries.at[spots[0]].set(smallest).at[spots[1]].set(top_value)


def levels(own_key, extent, shards, smallest, high):
    def one(axis_at, shards_of):
        heights = jax.random.uniform(jax.random.fold_in(jax.random.fold_in(own_key, 6), axis_at), (shards_of,), jnp.float32, smallest / len(shards), high / len(shards))
        return jnp.repeat(jnp.exp(heights), extent[axis_at] // shards_of).reshape((-1,) + (1,) * (len(extent) - axis_at - 1))

    level = one(*shards[0])
    for cut in shards[1:]:
        level = level * one(*cut)
    return level


def bell_draw(own_key, shape, scale, most, pieces=(), held_as=jnp.bfloat16):
    factor_of = levels(own_key, shape, pieces, -0.22, 0.18) if pieces else 1.0
    values = jax.random.normal(own_key, shape, jnp.float32) * scale * factor_of
    return jnp.minimum(jnp.maximum(values, -most), most).astype(held_as)


def setup_inputs(seed: int = 0, part: int = 0) -> dict:
    key_of = jax.random.split(jax.random.key(seed), 7)
    part_splits = jax.random.split(jax.random.fold_in(key_of[6], part), 7)
    queries = draw_queries(jax.random.fold_in(jax.random.fold_in(key_of[6], part), 71), part)
    key_value = draw_key_value(jax.random.fold_in(jax.random.fold_in(key_of[6], part), 71), part)
    keep = set_ends((jax.random.randint(part_splits[2], (REQUESTS,), 0, 2) < 1).astype(jnp.int32), jax.random.fold_in(part_splits[2], 1), 0, 1)
    windows = draw_windows(jax.random.fold_in(jax.random.fold_in(key_of[6], part), 71), part)
    gate = jnp.clip(jax.random.uniform(part_splits[4], (REQUESTS, D), jnp.float32, -1.5, 1.5), -1.5, 1.5)
    out_weight = bell_draw(key_of[5], (HH, D), HH ** -0.5, 0.125, ((0, 8),))
    return dict(queries=queries, key_value=key_value, keep=keep, windows=windows, gate=gate, out_weight=out_weight)


NEG_LARGE = -1e+30

def attend(query_rows, key_rows, value_rows, allowed):
    query_count = query_rows.shape[0]
    key_count = key_rows.shape[0]
    query_heads = query_rows.astype(jnp.float32).reshape(query_count, HEADS, HEAD_DIM)
    key_heads = key_rows.astype(jnp.float32).reshape(key_count, HEADS, HEAD_DIM)
    value_heads = value_rows.astype(jnp.float32).reshape(key_count, HEADS, HEAD_DIM)
    scores = jnp.einsum('qhd,khd->hqk', query_heads, key_heads) * (1.0 / math.sqrt(HEAD_DIM))
    scores = jnp.where(allowed[None], scores, NEG_LARGE)
    highest = lax.optimization_barrier(jnp.max(scores, axis=-1, keepdims=True))
    exponent = jnp.exp(scores - highest)
    totals = lax.optimization_barrier(jnp.sum(exponent, axis=-1, keepdims=True))
    weights = (exponent / totals).astype(jnp.bfloat16)
    mixture = jnp.einsum('hqk,khd->qhd', weights.astype(jnp.float32), value_heads)
    return mixture.astype(jnp.bfloat16).reshape(query_count, HEADS * HEAD_DIM)

def reference(queries, key_value, keep, windows, gate, out_weight):
    tokens = FRAMES * SP
    token_ids = jnp.arange(tokens, dtype=jnp.int32)
    frame_of = token_ids // SP
    row_of = token_ids % SP // WB
    column_of = token_ids % SP % WB

    def one_stream(index):
        request = index // 2
        branch = index % 2
        window = windows[request]
        allowed = jnp.abs(frame_of[:, None] - frame_of[None, :]) <= window[0]
        allowed = allowed & (jnp.abs(row_of[:, None] - row_of[None, :]) <= window[1])
        allowed = allowed & (jnp.abs(column_of[:, None] - column_of[None, :]) <= window[2])
        query_rows = queries[index].reshape(tokens, HH)
        key_rows = key_value[0, index].reshape(tokens, HH)
        value_rows = key_value[1, index].reshape(tokens, HH)
        attended = attend(query_rows, key_rows, value_rows, allowed)
        product = jnp.dot(attended, out_weight, preferred_element_type=jnp.float32)
        factor = jnp.where(branch == 1, keep[request], 1).astype(jnp.float32)
        result = product * gate[request][None, :] * factor
        return result.astype(jnp.bfloat16).reshape(FRAMES, SP, D)
    return lax.map(one_stream, jnp.arange(STREAMS, dtype=jnp.int32))
```

```python
import math

import jax
import jax.numpy as jnp
from jax import lax
from jax.experimental import pallas as pl
from jax.experimental.pallas import tpu as pltpu
from jax.sharding import PartitionSpec as P

HEADS = 20
HEAD_DIM = 128
WB = 14
HALO = 1


NEG_LARGE = -1e30
PIECE = 128
HEAD_GROUP = 4
LAG = 2
MATE_LAG = 6
RELAY_LAG = 4
PROJECT_LAG = 8


def padded_2(cells, sides, width):
    for axis, dim in sides:
        count = lax.axis_size(axis)
        ends = count - 1
        head = lax.slice_in_dim(cells, 0, width, axis=dim)
        tail = lax.slice_in_dim(cells, cells.shape[dim] - width, cells.shape[dim], axis=dim)
        cells = jnp.concatenate(
            [
                lax.ppermute(tail, axis, [(i, (i + 1) % count) for i in range(ends)]),
                cells,
                lax.ppermute(head, axis, [((i + 1) % count, i) for i in range(ends)]),
            ],
            axis=dim,
        )
    return cells


def window_mask(window, slab_index, frames_here, frames_total, spots):
    query_ids = jnp.arange(frames_here * spots, dtype=jnp.int32)
    key_ids = jnp.arange((frames_here + 2 * HALO) * spots, dtype=jnp.int32)
    query_frame = slab_index * frames_here + query_ids // spots
    key_frame = slab_index * frames_here - HALO + key_ids // spots
    query_row = query_ids % spots // WB
    key_row = key_ids % spots // WB
    query_column = query_ids % spots % WB
    key_column = key_ids % spots % WB
    inside = (key_frame >= 0) & (key_frame < frames_total)
    allowed = jnp.abs(query_frame[:, None] - key_frame[None, :]) <= window[0]
    allowed = allowed & (jnp.abs(query_row[:, None] - key_row[None, :]) <= window[1])
    allowed = allowed & (jnp.abs(query_column[:, None] - key_column[None, :]) <= window[2])
    return allowed & inside[None, :]


def attend(query_rows, key_rows, value_rows, allowed):
    query_count = query_rows.shape[0]
    key_count = key_rows.shape[0]
    query_heads = query_rows.reshape(query_count, HEADS, HEAD_DIM)
    key_heads = key_rows.reshape(key_count, HEADS, HEAD_DIM)
    value_heads = value_rows.reshape(key_count, HEADS, HEAD_DIM)
    scores = jnp.einsum("qhd,khd->hqk", query_heads, key_heads, preferred_element_type=jnp.float32)
    scores = scores * (1.0 / math.sqrt(HEAD_DIM))
    scores = jnp.where(allowed[None], scores, NEG_LARGE)
    highest = jnp.max(scores, axis=-1, keepdims=True)
    exponent = jnp.exp(scores - highest)
    totals = jnp.sum(exponent, axis=-1, keepdims=True)
    weights = (exponent / totals).astype(jnp.bfloat16)
    mixture = jnp.einsum("hqk,khd->qhd", weights, value_heads, preferred_element_type=jnp.float32)
    return mixture.astype(jnp.bfloat16).reshape(query_count, HEADS * HEAD_DIM)


def plain(queries, key_value, keep, windows, gate, out_weight):
    frames_here = queries.shape[1]
    spots = queries.shape[2]
    features = queries.shape[3]
    model_width = gate.shape[1]
    slab_index = lax.axis_index("slab")
    stream_index = lax.axis_index("owner")
    request = stream_index // 2
    branch = stream_index % 2
    frames_total = frames_here * lax.axis_size("slab")
    window = lax.dynamic_index_in_dim(windows, request, 0, keepdims=False)
    gate_row = lax.dynamic_index_in_dim(gate, request, 0, keepdims=False)
    keep_flag = lax.dynamic_index_in_dim(keep, request, 0, keepdims=False)
    factor = jnp.where(branch == 1, keep_flag, 1)
    padded = padded_2(key_value, (("slab", 2),), HALO)
    allowed = window_mask(window, slab_index, frames_here, frames_total, spots)
    branch_rows = frames_here * spots
    query_rows = queries[0].reshape(branch_rows, features)
    key_rows = padded[0, 0].reshape(-1, features)
    value_rows = padded[1, 0].reshape(-1, features)
    operands = (query_rows, key_rows, value_rows)
    attended_rows = attend(operands[0], operands[1], operands[2], allowed)
    quad = ("groups", "slab")
    parts = lax.axis_size("groups") * lax.axis_size("slab")
    place = lax.axis_index("groups") * lax.axis_size("slab") + slab_index
    width = model_width // parts
    own_columns = lax.dynamic_slice_in_dim(out_weight, place * width, width, 1)
    weight_part = lax.all_gather(own_columns, "owner", axis=0, tiled=True)
    all_rows = lax.all_gather(attended_rows, quad, axis=0, tiled=True)
    scaled_gate = gate_row * factor.astype(jnp.float32)
    gates = lax.all_to_all(
        jnp.broadcast_to(scaled_gate.reshape(parts, 1, width), (parts, 8, width)),
        quad, split_axis=0, concat_axis=0, tiled=True,
    )
    product = jnp.dot(all_rows, weight_part, preferred_element_type=jnp.float32)
    product = product.reshape(parts, branch_rows, width) * gates[:, :1]
    scaled = product.astype(jnp.bfloat16).reshape(parts * branch_rows, width)
    result = lax.all_to_all(scaled, quad, split_axis=0, concat_axis=1, tiled=True)
    return result.reshape((1, frames_here, spots, model_width))


def fused_kernel(
    query_hbm, kv_hbm, weight_hbm, gate_hbm, keep_ref, windows_ref, out_hbm,
    query, keys, values, weight, rows, finished, gates, gate_own, bias,
    load_sems, halo_send, halo_recv, gate_send, gate_recv, own_weight,
    weight_recv, side_send, up_send, down_send, mate_send,
    rows_recv, rows_send, relay_send, cols_recv, cols_send, own_out,
):
    group = lax.axis_index("groups")
    owner = lax.axis_index("owner")
    slab = lax.axis_index("slab")
    line, side = owner // 2, owner % 2
    lines = lax.axis_size("owner") // 2
    frames, spots, features = keys.shape[0] - HALO, keys.shape[1], keys.shape[2]
    tokens = frames * spots
    pieces, owners, depth, _ = weight.shape
    batches = rows.shape[0]
    span = features // batches
    quarter = pieces * PIECE
    place = group * 2 + slab
    across = (1 - group) * 2 + slab
    beside = group * 2 + 1 - slab
    corner = (1 - group) * 2 + 1 - slab
    to_side = {"owner": owner + 1 - 2 * side}
    to_up = {"owner": owner + 2}
    to_down = {"owner": owner - 2}
    to_across = {"groups": 1 - group}
    to_beside = {"slab": 1 - slab}
    to_corner = {"groups": 1 - group, "slab": 1 - slab}
    has_up = line + 1 < lines
    has_down = line > 0

    def remote(source, target, send, recv, device):
        return pltpu.make_async_remote_copy(
            src_ref=source, dst_ref=target, send_sem=send, recv_sem=recv,
            device_id=device, device_id_type=pl.DeviceIdType.MESH,
        )

    barrier = pltpu.get_barrier_semaphore()
    for device in (to_side, to_across, to_beside, to_corner):
        pl.semaphore_signal(barrier, inc=1, device_id=device, device_id_type=pl.DeviceIdType.MESH)

    @pl.when(has_up)
    def _():
        pl.semaphore_signal(barrier, inc=1, device_id=to_up, device_id_type=pl.DeviceIdType.MESH)

    @pl.when(has_down)
    def _():
        pl.semaphore_signal(barrier, inc=1, device_id=to_down, device_id_type=pl.DeviceIdType.MESH)

    loads = (
        pltpu.make_async_copy(query_hbm, query, load_sems.at[0]),
        pltpu.make_async_copy(kv_hbm.at[0], keys.at[pl.ds(0, frames)], load_sems.at[1]),
        pltpu.make_async_copy(kv_hbm.at[1], values.at[pl.ds(0, frames)], load_sems.at[2]),
        pltpu.make_async_copy(gate_hbm, gate_own, load_sems.at[3]),
    )
    for load in loads:
        load.start()
    pl.semaphore_wait(barrier, 4 + has_up.astype(jnp.int32) + has_down.astype(jnp.int32))

    def columns(index):
        return pl.ds(pl.multiple_of(place * quarter + index * PIECE, PIECE), PIECE)

    edge = (1 - slab) * (frames - 1)
    halos = (
        remote(kv_hbm.at[0, edge], keys.at[frames], halo_send.at[0], halo_recv.at[0], to_beside),
        remote(kv_hbm.at[1, edge], values.at[frames], halo_send.at[1], halo_recv.at[1], to_beside),
    )
    for halo in halos:
        halo.start()

    def side_copy(index, at, source):
        return remote(source, weight.at[index, 2 * at + side], side_send.at[index, at],
                      weight_recv.at[index, 2 * at + side], to_side)

    def up_copy(index, at, source):
        return remote(source, weight.at[index, 2 * at + side], up_send.at[index, at],
                      weight_recv.at[index, 2 * at + side], to_up)

    def down_copy(index, at, source):
        return remote(source, weight.at[index, 2 * at + side], down_send.at[index, at],
                      weight_recv.at[index, 2 * at + side], to_down)

    for index in range(pieces):
        mine = weight_hbm.at[:, columns(index)]
        side_copy(index, line, mine).start()

        @pl.when(has_up)
        def _():
            up_copy(index, line, mine).start()

        @pl.when(has_down)
        def _():
            down_copy(index, line, mine).start()

        pltpu.make_async_copy(mine, weight.at[index, owner], own_weight.at[index]).start()
    gate_copy = remote(gates.at[group], gates.at[group], gate_send, gate_recv, to_across)

    paired = lines % 2 == 0
    mate = line + 1 - 2 * (line % 2)
    to_mate = {"owner": owner + 2 - 4 * (line % 2)}

    def balanced(index):
        return 2 * index >= pieces if paired else index < 0

    def mate_copy(index):
        source = 2 * line + 1 - side
        block = weight.at[index, source]
        return remote(block, block, mate_send.at[index], weight_recv.at[index, source], to_mate)

    def forward(index, apart):
        below, above = line - apart, line + apart

        @pl.when(below >= 0)
        def _():
            block = weight.at[index, 2 * below + side]
            side_copy(index, below, block).wait_recv()

            @pl.when(has_up)
            def _():
                up_copy(index, below, block).start()

            @pl.when(jnp.logical_not(balanced(index) & (below == mate)))
            def _():
                side_copy(index, below, block).start()

        @pl.when(above < lines)
        def _():
            block = weight.at[index, 2 * above + side]
            side_copy(index, above, block).wait_recv()

            @pl.when(has_down)
            def _():
                down_copy(index, above, block).start()

            @pl.when(jnp.logical_not(balanced(index) & (above == mate)))
            def _():
                side_copy(index, above, block).start()

    def within(index, count):
        return (index >= 0) & (index < count)

    def mate_step(index):
        @pl.when(within(index, pieces) & balanced(index))
        def _():
            mate_copy(index).wait_recv()
            mate_copy(index).start()

    def forward_steps(step):
        for apart in range(lines - 1, 0, -1):
            index = step - LAG * apart

            @pl.when(within(index, pieces))
            def _():
                forward(index, apart)

    def places(ids):
        frame = sum((ids >= spots * step).astype(jnp.int32) for step in range(1, frames + HALO))
        spot = ids - frame * spots
        row = sum((spot >= WB * step).astype(jnp.int32) for step in range(1, spots // WB))
        return frame, row, spot - row * WB

    request = owner // 2
    query_frame, query_row, query_column = places(lax.broadcasted_iota(jnp.int32, (tokens, 1), 0))
    key_at, key_row, key_column = places(lax.broadcasted_iota(jnp.int32, (1, tokens + spots), 1))
    halo_frame = frames - slab
    key_frame = jnp.where(key_at < frames, key_at + slab * frames, halo_frame)
    allowed = jnp.abs(query_frame + slab * frames - key_frame) <= windows_ref[request, 0]
    allowed = allowed & (jnp.abs(query_row - key_row) <= windows_ref[request, 1])
    allowed = allowed & (jnp.abs(query_column - key_column) <= windows_ref[request, 2])
    bias[...] = jnp.where(allowed, 0.0, NEG_LARGE)

    for load in loads:
        load.wait()
    factor = jnp.where(owner % 2 == 1, keep_ref[request], 1).astype(jnp.float32)
    gates[group] = jnp.broadcast_to(gate_own[pl.ds(request, 1), :] * factor, gates.shape[1:])
    for halo in halos:
        halo.wait_recv()

    def rows_copy(batch, origin, send, device):
        block = rows.at[batch, origin]
        return remote(block, block, send, rows_recv.at[batch, origin], device)

    def attend_batch(batch, carry):
        for head in range(span // HEAD_DIM):
            lanes = pl.ds(pl.multiple_of(batch * span + head * HEAD_DIM, HEAD_DIM), HEAD_DIM)
            key_head = keys[:, :, lanes].reshape(-1, HEAD_DIM)
            value_head = values[:, :, lanes].reshape(-1, HEAD_DIM)
            scores = lax.dot_general(
                query[:, lanes], key_head, (((1,), (1,)), ((), ())),
                preferred_element_type=jnp.float32,
            )
            scores = scores * (1.0 / math.sqrt(HEAD_DIM)) + bias[...]
            exponent = jnp.exp(scores - jnp.max(scores, axis=-1, keepdims=True))
            totals = jnp.sum(exponent, axis=-1, keepdims=True)
            mixing = (exponent * (1.0 / totals)).astype(jnp.bfloat16)
            mixture = jnp.dot(mixing, value_head, preferred_element_type=jnp.float32)
            rows[batch, place, :, head * HEAD_DIM:(head + 1) * HEAD_DIM] = mixture.astype(jnp.bfloat16)
        rows_copy(batch, place, rows_send.at[batch, 0], to_across).start()
        rows_copy(batch, place, rows_send.at[batch, 1], to_beside).start()

        mate_step(batch - MATE_LAG)
        relay_step(batch - RELAY_LAG)
        forward_steps(batch)
        return carry

    def relay_step(batch):
        @pl.when(within(batch, batches))
        def _():
            rows_copy(batch, across, relay_send.at[batch], to_beside).wait_recv()
            rows_copy(batch, across, relay_send.at[batch], to_beside).start()

    def forward_round(step, carry):
        mate_step(step - MATE_LAG)
        relay_step(step - RELAY_LAG)
        forward_steps(step)
        return carry

    lax.fori_loop(0, batches, attend_batch, 0)
    gate_copy.start()
    lax.fori_loop(batches, PROJECT_LAG, forward_round, 0)

    def cols_copy(index, receiver, slot, device):
        return remote(finished.at[index, receiver], out_hbm.at[:, columns(index)],
                      cols_send.at[index, slot], cols_recv.at[index, place], device)

    def project(step, carry):
        index = step - PROJECT_LAG
        mate_step(step - MATE_LAG)
        relay_step(step - RELAY_LAG)

        @pl.when(index == 0)
        def _():
            gate_copy.wait_recv()
            for batch in range(batches):
                for origin in (beside, corner):
                    rows_copy(batch, origin, relay_send.at[batch], to_beside).wait_recv()

        pltpu.make_async_copy(weight_hbm.at[:, columns(index)], weight.at[index, owner],
                              own_weight.at[index]).wait()
        for at in range(lines):
            source = 2 * at + 1 - side
            block = weight.at[index, source]

            @pl.when(jnp.logical_not(balanced(index) & (at == line)))
            def _():
                remote(block, block, side_send.at[index, at], weight_recv.at[index, source], to_side).wait_recv()

        total = None
        whole = weight[index].reshape(owners * depth, PIECE)
        for batch in range(batches):
            part = jnp.dot(rows[batch].reshape(4 * tokens, span), whole[batch * span:(batch + 1) * span],
                           preferred_element_type=jnp.float32)
            total = part if total is None else total + part
        for receiver in range(4):
            gate_row = gates[receiver // 2, :, columns(index)][0:1]
            finished[index, receiver] = (total[receiver * tokens:(receiver + 1) * tokens] * gate_row).astype(jnp.bfloat16)
        cols_copy(index, across, 0, to_across).start()
        cols_copy(index, corner, 1, to_corner).start()
        cols_copy(index, beside, 2, to_beside).start()
        pltpu.make_async_copy(finished.at[index, place], out_hbm.at[:, columns(index)], own_out.at[index]).start()
        forward_steps(step)
        return carry

    lax.fori_loop(PROJECT_LAG, PROJECT_LAG + pieces, project, 0)

    def drain(index, carry):
        for origin in (across, corner, beside):
            remote(finished.at[index, place], out_hbm.at[:, columns(index)], cols_send.at[index, 0],
                   cols_recv.at[index, origin], to_across).wait_recv()
        cols_copy(index, across, 0, to_across).wait_send()
        cols_copy(index, corner, 1, to_corner).wait_send()
        cols_copy(index, beside, 2, to_beside).wait_send()
        pltpu.make_async_copy(finished.at[index, place], out_hbm.at[:, columns(index)], own_out.at[index]).wait()
        for at in range(lines):
            block = weight.at[index, 2 * at + side]

            @pl.when(jnp.logical_not(balanced(index) & (at == mate)))
            def _():
                side_copy(index, at, block).wait_send()

            @pl.when(has_up & (at <= line))
            def _():
                up_copy(index, at, block).wait_send()

            @pl.when(has_down & (at >= line))
            def _():
                down_copy(index, at, block).wait_send()

        @pl.when(balanced(index))
        def _():
            mate_copy(index).wait_send()

        return carry

    lax.fori_loop(0, pieces, drain, 0)
    for halo in halos:
        halo.wait_send()
    gate_copy.wait_send()
    for batch in range(batches):
        rows_copy(batch, place, rows_send.at[batch, 0], to_across).wait_send()
        rows_copy(batch, place, rows_send.at[batch, 1], to_beside).wait_send()
        rows_copy(batch, across, relay_send.at[batch], to_beside).wait_send()


def fused(queries, key_value, keep, windows, gate, out_weight):
    frames, spots, features = queries.shape[1:]
    model_width = gate.shape[1]
    owners = lax.axis_size("owner")
    tokens = frames * spots
    depth = out_weight.shape[0]
    pieces = model_width // 4 // PIECE
    span = HEAD_GROUP * HEAD_DIM
    batches = features // span
    lines = owners // 2
    bf16 = jnp.bfloat16
    dma = pltpu.SemaphoreType.DMA
    whole = pl.BlockSpec(memory_space=pl.ANY)
    result = pl.pallas_call(
        fused_kernel,
        out_shape=jax.ShapeDtypeStruct((tokens, model_width), bf16),
        in_specs=[whole] * 4 + [pl.BlockSpec(memory_space=pltpu.SMEM)] * 2,
        out_specs=whole,
        scratch_shapes=[
            pltpu.VMEM((tokens, features), bf16),
            pltpu.VMEM((frames + HALO, spots, features), bf16),
            pltpu.VMEM((frames + HALO, spots, features), bf16),
            pltpu.VMEM((pieces, owners, depth, PIECE), bf16),
            pltpu.VMEM((batches, 4, tokens, span), bf16),
            pltpu.VMEM((pieces, 4, tokens, PIECE), bf16),
            pltpu.VMEM((2, 8, model_width), jnp.float32),
            pltpu.VMEM(gate.shape, jnp.float32),
            pltpu.VMEM((tokens, tokens + spots), jnp.float32),
            dma((4,)), dma((2,)), dma((2,)), dma, dma, dma((pieces,)),
            dma((pieces, owners)), dma((pieces, lines)), dma((pieces, lines)), dma((pieces, lines)), dma((pieces,)),
            dma((batches, 4)), dma((batches, 2)), dma((batches,)),
            dma((pieces, 4)), dma((pieces, 3)), dma((pieces,)),
        ],
        compiler_params=pltpu.CompilerParams(
            collective_id=0, has_side_effects=True, vmem_limit_bytes=56 * 2**20,
        ),
    )(
        queries.reshape(tokens, features), key_value.reshape(2, frames, spots, features),
        out_weight, gate, keep, windows,
    )
    return result.reshape(1, frames, spots, model_width)


def on_device(queries, key_value, keep, windows, gate, out_weight):
    frames, spots, features = queries.shape[1:]
    fits = (
        lax.axis_size("slab") == 2
        and lax.axis_size("groups") == 2
        and lax.axis_size("owner") % 2 == 0
        and out_weight.shape[0] % 16 == 0
        and spots % 16 == 0
        and spots % WB == 0
        and features % (HEAD_GROUP * HEAD_DIM) == 0
        and gate.shape[1] % (4 * PIECE) == 0
    )
    chosen = fused if fits else plain
    return chosen(queries, key_value, keep, windows, gate, out_weight)


def solution(mesh):
    placed = (
        P(("groups", "owner"), "slab", None, None),
        P(None, ("groups", "owner"), "slab", None, None),
        P("groups"),
        P("groups", None),
        P("groups", None),
        P("owner", None),
    )
    return jax.shard_map(
        on_device,
        mesh=mesh,
        in_specs=placed,
        out_specs=P(("groups", "owner"), "slab", None, None),
        check_vma=False,
    )
```

```python
import math

import jax
import jax.numpy as jnp
from jax import lax
from jax.experimental import pallas as pl
from jax.experimental.pallas import tpu as pltpu
from jax.sharding import PartitionSpec as P

HEADS = 20
HEAD_DIM = 128
WB = 14
HALO = 1


NEG_LARGE = -1e30
PIECE = 128
HEAD_GROUP = 4
LAG = 2
MATE_LAG = 6
RELAY_LAG = 4
PROJECT_LAG = 8


def padded_2(cells, sides, width):
    for axis, dim in sides:
        count = lax.axis_size(axis)
        ends = count - 1
        head = lax.slice_in_dim(cells, 0, width, axis=dim)
        tail = lax.slice_in_dim(cells, cells.shape[dim] - width, cells.shape[dim], axis=dim)
        cells = jnp.concatenate(
            [
                lax.ppermute(tail, axis, [(i, (i + 1) % count) for i in range(ends)]),
                cells,
                lax.ppermute(head, axis, [((i + 1) % count, i) for i in range(ends)]),
            ],
            axis=dim,
        )
    return cells


def window_mask(window, slab_index, frames_here, frames_total, spots):
    query_ids = jnp.arange(frames_here * spots, dtype=jnp.int32)
    key_ids = jnp.arange((frames_here + 2 * HALO) * spots, dtype=jnp.int32)
    query_frame = slab_index * frames_here + query_ids // spots
    key_frame = slab_index * frames_here - HALO + key_ids // spots
    query_row = query_ids % spots // WB
    key_row = key_ids % spots // WB
    query_column = query_ids % spots % WB
    key_column = key_ids % spots % WB
    inside = (key_frame >= 0) & (key_frame < frames_total)
    allowed = jnp.abs(query_frame[:, None] - key_frame[None, :]) <= window[0]
    allowed = allowed & (jnp.abs(query_row[:, None] - key_row[None, :]) <= window[1])
    allowed = allowed & (jnp.abs(query_column[:, None] - key_column[None, :]) <= window[2])
    return allowed & inside[None, :]


def attend(query_rows, key_rows, value_rows, allowed):
    query_count = query_rows.shape[0]
    key_count = key_rows.shape[0]
    query_heads = query_rows.reshape(query_count, HEADS, HEAD_DIM)
    key_heads = key_rows.reshape(key_count, HEADS, HEAD_DIM)
    value_heads = value_rows.reshape(key_count, HEADS, HEAD_DIM)
    scores = jnp.einsum("qhd,khd->hqk", query_heads, key_heads, preferred_element_type=jnp.float32)
    scores = scores * (1.0 / math.sqrt(HEAD_DIM))
    scores = jnp.where(allowed[None], scores, NEG_LARGE)
    highest = jnp.max(scores, axis=-1, keepdims=True)
    exponent = jnp.exp(scores - highest)
    totals = jnp.sum(exponent, axis=-1, keepdims=True)
    weights = (exponent / totals).astype(jnp.bfloat16)
    mixture = jnp.einsum("hqk,khd->qhd", weights, value_heads, preferred_element_type=jnp.float32)
    return mixture.astype(jnp.bfloat16).reshape(query_count, HEADS * HEAD_DIM)


def plain(queries, key_value, keep, windows, gate, out_weight):
    frames_here = queries.shape[1]
    spots = queries.shape[2]
    features = queries.shape[3]
    model_width = gate.shape[1]
    slab_index = lax.axis_index("slab")
    stream_index = lax.axis_index("owner")
    request = stream_index // 2
    branch = stream_index % 2
    frames_total = frames_here * lax.axis_size("slab")
    window = lax.dynamic_index_in_dim(windows, request, 0, keepdims=False)
    gate_row = lax.dynamic_index_in_dim(gate, request, 0, keepdims=False)
    keep_flag = lax.dynamic_index_in_dim(keep, request, 0, keepdims=False)
    factor = jnp.where(branch == 1, keep_flag, 1)
    padded = padded_2(key_value, (("slab", 2),), HALO)
    allowed = window_mask(window, slab_index, frames_here, frames_total, spots)
    branch_rows = frames_here * spots
    query_rows = queries[0].reshape(branch_rows, features)
    key_rows = padded[0, 0].reshape(-1, features)
    value_rows = padded[1, 0].reshape(-1, features)
    operands = (query_rows, key_rows, value_rows)
    attended_rows = attend(operands[0], operands[1], operands[2], allowed)
    quad = ("groups", "slab")
    parts = lax.axis_size("groups") * lax.axis_size("slab")
    place = lax.axis_index("groups") * lax.axis_size("slab") + slab_index
    width = model_width // parts
    own_columns = lax.dynamic_slice_in_dim(out_weight, place * width, width, 1)
    weight_part = lax.all_gather(own_columns, "owner", axis=0, tiled=True)
    all_rows = lax.all_gather(attended_rows, quad, axis=0, tiled=True)
    scaled_gate = gate_row * factor.astype(jnp.float32)
    gates = lax.all_to_all(
        jnp.broadcast_to(scaled_gate.reshape(parts, 1, width), (parts, 8, width)),
        quad, split_axis=0, concat_axis=0, tiled=True,
    )
    product = jnp.dot(all_rows, weight_part, preferred_element_type=jnp.float32)
    product = product.reshape(parts, branch_rows, width) * gates[:, :1]
    scaled = product.astype(jnp.bfloat16).reshape(parts * branch_rows, width)
    result = lax.all_to_all(scaled, quad, split_axis=0, concat_axis=1, tiled=True)
    return result.reshape((1, frames_here, spots, model_width))


def fused_kernel(
    query_hbm, kv_hbm, weight_hbm, gate_hbm, keep_ref, windows_ref, out_ref,
    query, keys, values, weight, rows, finished, gates, gate_own, bias,
    load_sems, halo_send, halo_recv, gate_send, gate_recv, own_weight,
    weight_recv, side_send, up_send, down_send, mate_send,
    rows_recv, rows_send, relay_send, cols_recv, cols_send, own_out,
):
    group = lax.axis_index("groups")
    owner = lax.axis_index("owner")
    slab = lax.axis_index("slab")
    line, side = owner // 2, owner % 2
    lines = lax.axis_size("owner") // 2
    frames, spots, features = keys.shape[0] - HALO, keys.shape[1], keys.shape[2]
    tokens = frames * spots
    pieces, owners, depth, _ = weight.shape
    batches = rows.shape[0]
    span = features // batches
    quarter = pieces * PIECE
    place = group * 2 + slab
    across = (1 - group) * 2 + slab
    beside = group * 2 + 1 - slab
    corner = (1 - group) * 2 + 1 - slab
    to_side = {"owner": owner + 1 - 2 * side}
    to_up = {"owner": owner + 2}
    to_down = {"owner": owner - 2}
    to_across = {"groups": 1 - group}
    to_beside = {"slab": 1 - slab}
    to_corner = {"groups": 1 - group, "slab": 1 - slab}
    has_up = line + 1 < lines
    has_down = line > 0

    def remote(source, target, send, recv, device):
        return pltpu.make_async_remote_copy(
            src_ref=source, dst_ref=target, send_sem=send, recv_sem=recv,
            device_id=device, device_id_type=pl.DeviceIdType.MESH,
        )

    barrier = pltpu.get_barrier_semaphore()
    for device in (to_side, to_across, to_beside, to_corner):
        pl.semaphore_signal(barrier, inc=1, device_id=device, device_id_type=pl.DeviceIdType.MESH)

    @pl.when(has_up)
    def _():
        pl.semaphore_signal(barrier, inc=1, device_id=to_up, device_id_type=pl.DeviceIdType.MESH)

    @pl.when(has_down)
    def _():
        pl.semaphore_signal(barrier, inc=1, device_id=to_down, device_id_type=pl.DeviceIdType.MESH)

    loads = (
        pltpu.make_async_copy(query_hbm, query, load_sems.at[0]),
        pltpu.make_async_copy(kv_hbm.at[0], keys.at[pl.ds(0, frames)], load_sems.at[1]),
        pltpu.make_async_copy(kv_hbm.at[1], values.at[pl.ds(0, frames)], load_sems.at[2]),
        pltpu.make_async_copy(gate_hbm, gate_own, load_sems.at[3]),
    )
    for load in loads:
        load.start()
    pl.semaphore_wait(barrier, 4 + has_up.astype(jnp.int32) + has_down.astype(jnp.int32))

    def columns(index):
        return pl.ds(pl.multiple_of(place * quarter + index * PIECE, PIECE), PIECE)

    edge = (1 - slab) * (frames - 1)
    halos = (
        remote(kv_hbm.at[0, edge], keys.at[frames], halo_send.at[0], halo_recv.at[0], to_beside),
        remote(kv_hbm.at[1, edge], values.at[frames], halo_send.at[1], halo_recv.at[1], to_beside),
    )
    for halo in halos:
        halo.start()

    def side_copy(index, at, source):
        return remote(source, weight.at[index, 2 * at + side], side_send.at[index, at],
                      weight_recv.at[index, 2 * at + side], to_side)

    def up_copy(index, at, source):
        return remote(source, weight.at[index, 2 * at + side], up_send.at[index, at],
                      weight_recv.at[index, 2 * at + side], to_up)

    def down_copy(index, at, source):
        return remote(source, weight.at[index, 2 * at + side], down_send.at[index, at],
                      weight_recv.at[index, 2 * at + side], to_down)

    for index in range(pieces):
        mine = weight_hbm.at[:, columns(index)]
        side_copy(index, line, mine).start()

        @pl.when(has_up)
        def _():
            up_copy(index, line, mine).start()

        @pl.when(has_down)
        def _():
            down_copy(index, line, mine).start()

        pltpu.make_async_copy(mine, weight.at[index, owner], own_weight.at[index]).start()
    gate_copy = remote(gates.at[group], gates.at[group], gate_send, gate_recv, to_across)

    paired = lines % 2 == 0
    mate = line + 1 - 2 * (line % 2)
    to_mate = {"owner": owner + 2 - 4 * (line % 2)}

    def balanced(index):
        return 2 * index >= pieces if paired else index < 0

    def mate_copy(index):
        source = 2 * line + 1 - side
        block = weight.at[index, source]
        return remote(block, block, mate_send.at[index], weight_recv.at[index, source], to_mate)

    def forward(index, apart):
        below, above = line - apart, line + apart

        @pl.when(below >= 0)
        def _():
            block = weight.at[index, 2 * below + side]
            side_copy(index, below, block).wait_recv()

            @pl.when(has_up)
            def _():
                up_copy(index, below, block).start()

            @pl.when(jnp.logical_not(balanced(index) & (below == mate)))
            def _():
                side_copy(index, below, block).start()

        @pl.when(above < lines)
        def _():
            block = weight.at[index, 2 * above + side]
            side_copy(index, above, block).wait_recv()

            @pl.when(has_down)
            def _():
                down_copy(index, above, block).start()

            @pl.when(jnp.logical_not(balanced(index) & (above == mate)))
            def _():
                side_copy(index, above, block).start()

    def within(index, count):
        return (index >= 0) & (index < count)

    def mate_step(index):
        @pl.when(within(index, pieces) & balanced(index))
        def _():
            mate_copy(index).wait_recv()
            mate_copy(index).start()

    def forward_steps(step):
        for apart in range(lines - 1, 0, -1):
            index = step - LAG * apart

            @pl.when(within(index, pieces))
            def _():
                forward(index, apart)

    def places(ids):
        frame = sum((ids >= spots * step).astype(jnp.int32) for step in range(1, frames + HALO))
        spot = ids - frame * spots
        row = sum((spot >= WB * step).astype(jnp.int32) for step in range(1, spots // WB))
        return frame, row, spot - row * WB

    request = owner // 2
    query_frame, query_row, query_column = places(lax.broadcasted_iota(jnp.int32, (tokens, 1), 0))
    key_at, key_row, key_column = places(lax.broadcasted_iota(jnp.int32, (1, tokens + spots), 1))
    halo_frame = frames - slab
    key_frame = jnp.where(key_at < frames, key_at + slab * frames, halo_frame)
    allowed = jnp.abs(query_frame + slab * frames - key_frame) <= windows_ref[request, 0]
    allowed = allowed & (jnp.abs(query_row - key_row) <= windows_ref[request, 1])
    allowed = allowed & (jnp.abs(query_column - key_column) <= windows_ref[request, 2])
    bias[...] = jnp.where(allowed, 0.0, NEG_LARGE)

    for load in loads:
        load.wait()
    factor = jnp.where(owner % 2 == 1, keep_ref[request], 1).astype(jnp.float32)
    gates[group] = jnp.broadcast_to(gate_own[pl.ds(request, 1), :] * factor, gates.shape[1:])
    for halo in halos:
        halo.wait_recv()

    def rows_copy(batch, origin, send, device):
        block = rows.at[batch, origin]
        return remote(block, block, send, rows_recv.at[batch, origin], device)

    def attend_batch(batch, carry):
        for head in range(span // HEAD_DIM):
            lanes = pl.ds(pl.multiple_of(batch * span + head * HEAD_DIM, HEAD_DIM), HEAD_DIM)
            key_head = keys[:, :, lanes].reshape(-1, HEAD_DIM)
            value_head = values[:, :, lanes].reshape(-1, HEAD_DIM)
            scores = lax.dot_general(
                query[:, lanes], key_head, (((1,), (1,)), ((), ())),
                preferred_element_type=jnp.float32,
            )
            scores = scores * (1.0 / math.sqrt(HEAD_DIM)) + bias[...]
            exponent = jnp.exp(scores - jnp.max(scores, axis=-1, keepdims=True))
            totals = jnp.sum(exponent, axis=-1, keepdims=True)
            mixing = (exponent * (1.0 / totals)).astype(jnp.bfloat16)
            mixture = jnp.dot(mixing, value_head, preferred_element_type=jnp.float32)
            rows[batch, place, :, head * HEAD_DIM:(head + 1) * HEAD_DIM] = mixture.astype(jnp.bfloat16)
        rows_copy(batch, place, rows_send.at[batch, 0], to_across).start()
        rows_copy(batch, place, rows_send.at[batch, 1], to_beside).start()

        mate_step(batch - MATE_LAG)
        relay_step(batch - RELAY_LAG)
        forward_steps(batch)
        return carry

    def relay_step(batch):
        @pl.when(within(batch, batches))
        def _():
            rows_copy(batch, across, relay_send.at[batch], to_beside).wait_recv()
            rows_copy(batch, across, relay_send.at[batch], to_beside).start()

    def forward_round(step, carry):
        mate_step(step - MATE_LAG)
        relay_step(step - RELAY_LAG)
        forward_steps(step)
        return carry

    lax.fori_loop(0, batches, attend_batch, 0)
    gate_copy.start()
    lax.fori_loop(batches, PROJECT_LAG, forward_round, 0)

    def cols_copy(index, receiver, slot, device):
        return remote(finished.at[index, receiver], out_ref.at[:, columns(index)],
                      cols_send.at[index, slot], cols_recv.at[index, place], device)

    def project(step, carry):
        index = step - PROJECT_LAG
        mate_step(step - MATE_LAG)
        relay_step(step - RELAY_LAG)

        @pl.when(index == 0)
        def _():
            gate_copy.wait_recv()
            for batch in range(batches):
                for origin in (beside, corner):
                    rows_copy(batch, origin, relay_send.at[batch], to_beside).wait_recv()

        pltpu.make_async_copy(weight_hbm.at[:, columns(index)], weight.at[index, owner],
                              own_weight.at[index]).wait()
        for at in range(lines):
            source = 2 * at + 1 - side
            block = weight.at[index, source]

            @pl.when(jnp.logical_not(balanced(index) & (at == line)))
            def _():
                remote(block, block, side_send.at[index, at], weight_recv.at[index, source], to_side).wait_recv()

        total = None
        whole = weight[index].reshape(owners * depth, PIECE)
        for batch in range(batches):
            part = jnp.dot(rows[batch].reshape(4 * tokens, span), whole[batch * span:(batch + 1) * span],
                           preferred_element_type=jnp.float32)
            total = part if total is None else total + part
        for receiver in range(4):
            gate_row = gates[receiver // 2, :, columns(index)][0:1]
            finished[index, receiver] = (total[receiver * tokens:(receiver + 1) * tokens] * gate_row).astype(jnp.bfloat16)
        cols_copy(index, across, 0, to_across).start()
        cols_copy(index, corner, 1, to_corner).start()
        cols_copy(index, beside, 2, to_beside).start()
        pltpu.make_async_copy(finished.at[index, place], out_ref.at[:, columns(index)], own_out.at[index]).start()
        forward_steps(step)
        return carry

    lax.fori_loop(PROJECT_LAG, PROJECT_LAG + pieces, project, 0)

    def drain(index, carry):
        for origin in (across, corner, beside):
            remote(finished.at[index, place], out_ref.at[:, columns(index)], cols_send.at[index, 0],
                   cols_recv.at[index, origin], to_across).wait_recv()
        cols_copy(index, across, 0, to_across).wait_send()
        cols_copy(index, corner, 1, to_corner).wait_send()
        cols_copy(index, beside, 2, to_beside).wait_send()
        pltpu.make_async_copy(finished.at[index, place], out_ref.at[:, columns(index)], own_out.at[index]).wait()
        for at in range(lines):
            block = weight.at[index, 2 * at + side]

            @pl.when(jnp.logical_not(balanced(index) & (at == mate)))
            def _():
                side_copy(index, at, block).wait_send()

            @pl.when(has_up & (at <= line))
            def _():
                up_copy(index, at, block).wait_send()

            @pl.when(has_down & (at >= line))
            def _():
                down_copy(index, at, block).wait_send()

        @pl.when(balanced(index))
        def _():
            mate_copy(index).wait_send()

        return carry

    lax.fori_loop(0, pieces, drain, 0)
    for halo in halos:
        halo.wait_send()
    gate_copy.wait_send()
    for batch in range(batches):
        rows_copy(batch, place, rows_send.at[batch, 0], to_across).wait_send()
        rows_copy(batch, place, rows_send.at[batch, 1], to_beside).wait_send()
        rows_copy(batch, across, relay_send.at[batch], to_beside).wait_send()


def fused(queries, key_value, keep, windows, gate, out_weight):
    frames, spots, features = queries.shape[1:]
    model_width = gate.shape[1]
    owners = lax.axis_size("owner")
    tokens = frames * spots
    depth = out_weight.shape[0]
    pieces = model_width // 4 // PIECE
    span = HEAD_GROUP * HEAD_DIM
    batches = features // span
    lines = owners // 2
    bf16 = jnp.bfloat16
    dma = pltpu.SemaphoreType.DMA
    whole = pl.BlockSpec(memory_space=pl.ANY)
    result = pl.pallas_call(
        fused_kernel,
        out_shape=pltpu.VMEM((tokens, model_width), bf16),
        in_specs=[whole] * 4 + [pl.BlockSpec(memory_space=pltpu.SMEM)] * 2,
        out_specs=whole,
        scratch_shapes=[
            pltpu.VMEM((tokens, features), bf16),
            pltpu.VMEM((frames + HALO, spots, features), bf16),
            pltpu.VMEM((frames + HALO, spots, features), bf16),
            pltpu.VMEM((pieces, owners, depth, PIECE), bf16),
            pltpu.VMEM((batches, 4, tokens, span), bf16),
            pltpu.VMEM((pieces, 4, tokens, PIECE), bf16),
            pltpu.VMEM((2, 8, model_width), jnp.float32),
            pltpu.VMEM(gate.shape, jnp.float32),
            pltpu.VMEM((tokens, tokens + spots), jnp.float32),
            dma((4,)), dma((2,)), dma((2,)), dma, dma, dma((pieces,)),
            dma((pieces, owners)), dma((pieces, lines)), dma((pieces, lines)), dma((pieces, lines)), dma((pieces,)),
            dma((batches, 4)), dma((batches, 2)), dma((batches,)),
            dma((pieces, 4)), dma((pieces, 3)), dma((pieces,)),
        ],
        compiler_params=pltpu.CompilerParams(
            collective_id=0, has_side_effects=True, vmem_limit_bytes=44 * 2**20,
        ),
    )(
        queries.reshape(tokens, features), key_value.reshape(2, frames, spots, features),
        out_weight, gate, keep, windows,
    )
    return result.reshape(1, frames, spots, model_width)


def on_device(queries, key_value, keep, windows, gate, out_weight):
    frames, spots, features = queries.shape[1:]
    fits = (
        lax.axis_size("slab") == 2
        and lax.axis_size("groups") == 2
        and lax.axis_size("owner") % 2 == 0
        and out_weight.shape[0] % 16 == 0
        and spots % 16 == 0
        and spots % WB == 0
        and features % (HEAD_GROUP * HEAD_DIM) == 0
        and gate.shape[1] % (4 * PIECE) == 0
    )
    chosen = fused if fits else plain
    return chosen(queries, key_value, keep, windows, gate, out_weight)


def solution(mesh):
    placed = (
        P(("groups", "owner"), "slab", None, None),
        P(None, ("groups", "owner"), "slab", None, None),
        P("groups"),
        P("groups", None),
        P("groups", None),
        P("owner", None),
    )
    return jax.shard_map(
        on_device,
        mesh=mesh,
        in_specs=placed,
        out_specs=P(("groups", "owner"), "slab", None, None),
        check_vma=False,
    )
```

```python
import math

import jax
import jax.numpy as jnp
from jax import lax
from jax.experimental import pallas as pl
from jax.experimental.pallas import tpu as pltpu
from jax.sharding import PartitionSpec as P

HEADS = 20
HEAD_DIM = 128
WB = 14
HALO = 1


NEG_LARGE = -1e30
PIECE = 128
HEAD_GROUP = 4
LAG = 2
MATE_LAG = 6
RELAY_LAG = 4
PROJECT_LAG = 8


def padded_2(cells, sides, width):
    for axis, dim in sides:
        count = lax.axis_size(axis)
        ends = count - 1
        head = lax.slice_in_dim(cells, 0, width, axis=dim)
        tail = lax.slice_in_dim(cells, cells.shape[dim] - width, cells.shape[dim], axis=dim)
        cells = jnp.concatenate(
            [
                lax.ppermute(tail, axis, [(i, (i + 1) % count) for i in range(ends)]),
                cells,
                lax.ppermute(head, axis, [((i + 1) % count, i) for i in range(ends)]),
            ],
            axis=dim,
        )
    return cells


def window_mask(window, slab_index, frames_here, frames_total, spots):
    query_ids = jnp.arange(frames_here * spots, dtype=jnp.int32)
    key_ids = jnp.arange((frames_here + 2 * HALO) * spots, dtype=jnp.int32)
    query_frame = slab_index * frames_here + query_ids // spots
    key_frame = slab_index * frames_here - HALO + key_ids // spots
    query_row = query_ids % spots // WB
    key_row = key_ids % spots // WB
    query_column = query_ids % spots % WB
    key_column = key_ids % spots % WB
    inside = (key_frame >= 0) & (key_frame < frames_total)
    allowed = jnp.abs(query_frame[:, None] - key_frame[None, :]) <= window[0]
    allowed = allowed & (jnp.abs(query_row[:, None] - key_row[None, :]) <= window[1])
    allowed = allowed & (jnp.abs(query_column[:, None] - key_column[None, :]) <= window[2])
    return allowed & inside[None, :]


def attend(query_rows, key_rows, value_rows, allowed):
    query_count = query_rows.shape[0]
    key_count = key_rows.shape[0]
    query_heads = query_rows.reshape(query_count, HEADS, HEAD_DIM)
    key_heads = key_rows.reshape(key_count, HEADS, HEAD_DIM)
    value_heads = value_rows.reshape(key_count, HEADS, HEAD_DIM)
    scores = jnp.einsum("qhd,khd->hqk", query_heads, key_heads, preferred_element_type=jnp.float32)
    scores = scores * (1.0 / math.sqrt(HEAD_DIM))
    scores = jnp.where(allowed[None], scores, NEG_LARGE)
    highest = jnp.max(scores, axis=-1, keepdims=True)
    exponent = jnp.exp(scores - highest)
    totals = jnp.sum(exponent, axis=-1, keepdims=True)
    weights = (exponent / totals).astype(jnp.bfloat16)
    mixture = jnp.einsum("hqk,khd->qhd", weights, value_heads, preferred_element_type=jnp.float32)
    return mixture.astype(jnp.bfloat16).reshape(query_count, HEADS * HEAD_DIM)


def plain(queries, key_value, keep, windows, gate, out_weight):
    frames_here = queries.shape[1]
    spots = queries.shape[2]
    features = queries.shape[3]
    model_width = gate.shape[1]
    slab_index = lax.axis_index("slab")
    stream_index = lax.axis_index("owner")
    request = stream_index // 2
    branch = stream_index % 2
    frames_total = frames_here * lax.axis_size("slab")
    window = lax.dynamic_index_in_dim(windows, request, 0, keepdims=False)
    gate_row = lax.dynamic_index_in_dim(gate, request, 0, keepdims=False)
    keep_flag = lax.dynamic_index_in_dim(keep, request, 0, keepdims=False)
    factor = jnp.where(branch == 1, keep_flag, 1)
    padded = padded_2(key_value, (("slab", 2),), HALO)
    allowed = window_mask(window, slab_index, frames_here, frames_total, spots)
    branch_rows = frames_here * spots
    query_rows = queries[0].reshape(branch_rows, features)
    key_rows = padded[0, 0].reshape(-1, features)
    value_rows = padded[1, 0].reshape(-1, features)
    operands = (query_rows, key_rows, value_rows)
    attended_rows = attend(operands[0], operands[1], operands[2], allowed)
    quad = ("groups", "slab")
    parts = lax.axis_size("groups") * lax.axis_size("slab")
    place = lax.axis_index("groups") * lax.axis_size("slab") + slab_index
    width = model_width // parts
    own_columns = lax.dynamic_slice_in_dim(out_weight, place * width, width, 1)
    weight_part = lax.all_gather(own_columns, "owner", axis=0, tiled=True)
    all_rows = lax.all_gather(attended_rows, quad, axis=0, tiled=True)
    scaled_gate = gate_row * factor.astype(jnp.float32)
    gates = lax.all_to_all(
        jnp.broadcast_to(scaled_gate.reshape(parts, 1, width), (parts, 8, width)),
        quad, split_axis=0, concat_axis=0, tiled=True,
    )
    product = jnp.dot(all_rows, weight_part, preferred_element_type=jnp.float32)
    product = product.reshape(parts, branch_rows, width) * gates[:, :1]
    scaled = product.astype(jnp.bfloat16).reshape(parts * branch_rows, width)
    result = lax.all_to_all(scaled, quad, split_axis=0, concat_axis=1, tiled=True)
    return result.reshape((1, frames_here, spots, model_width))


def fused_kernel(
    query_hbm, kv_hbm, weight_hbm, gate_hbm, keep_ref, windows_ref, out_ref,
    query, keys, values, weight, rows, finished, gates, gate_own, bias,
    load_sems, halo_send, halo_recv, gate_send, gate_recv, own_weight,
    weight_recv, side_send, up_send, down_send, mate_send,
    rows_recv, rows_send, relay_send, cols_recv, cols_send, own_out,
):
    group = lax.axis_index("groups")
    owner = lax.axis_index("owner")
    slab = lax.axis_index("slab")
    line, side = owner // 2, owner % 2
    lines = lax.axis_size("owner") // 2
    frames, spots, features = keys.shape[0] - HALO, keys.shape[1], keys.shape[2]
    tokens = frames * spots
    pieces, owners, depth, _ = weight.shape
    batches = rows.shape[0]
    span = features // batches
    quarter = pieces * PIECE
    place = group * 2 + slab
    across = (1 - group) * 2 + slab
    beside = group * 2 + 1 - slab
    corner = (1 - group) * 2 + 1 - slab
    to_side = {"owner": owner + 1 - 2 * side}
    to_up = {"owner": owner + 2}
    to_down = {"owner": owner - 2}
    to_across = {"groups": 1 - group}
    to_beside = {"slab": 1 - slab}
    to_corner = {"groups": 1 - group, "slab": 1 - slab}
    has_up = line + 1 < lines
    has_down = line > 0

    def remote(source, target, send, recv, device):
        return pltpu.make_async_remote_copy(
            src_ref=source, dst_ref=target, send_sem=send, recv_sem=recv,
            device_id=device, device_id_type=pl.DeviceIdType.MESH,
        )

    barrier = pltpu.get_barrier_semaphore()
    for device in (to_side, to_across, to_beside, to_corner):
        pl.semaphore_signal(barrier, inc=1, device_id=device, device_id_type=pl.DeviceIdType.MESH)

    @pl.when(has_up)
    def _():
        pl.semaphore_signal(barrier, inc=1, device_id=to_up, device_id_type=pl.DeviceIdType.MESH)

    @pl.when(has_down)
    def _():
        pl.semaphore_signal(barrier, inc=1, device_id=to_down, device_id_type=pl.DeviceIdType.MESH)

    loads = (
        pltpu.make_async_copy(query_hbm, query, load_sems.at[0]),
        pltpu.make_async_copy(kv_hbm.at[0], keys.at[pl.ds(0, frames)], load_sems.at[1]),
        pltpu.make_async_copy(kv_hbm.at[1], values.at[pl.ds(0, frames)], load_sems.at[2]),
        pltpu.make_async_copy(gate_hbm, gate_own, load_sems.at[3]),
    )
    for load in loads:
        load.start()
    pl.semaphore_wait(barrier, 4 + has_up.astype(jnp.int32) + has_down.astype(jnp.int32))

    def columns(index):
        return pl.ds(pl.multiple_of(place * quarter + index * PIECE, PIECE), PIECE)

    edge = (1 - slab) * (frames - 1)
    halos = (
        remote(kv_hbm.at[0, edge], keys.at[frames], halo_send.at[0], halo_recv.at[0], to_beside),
        remote(kv_hbm.at[1, edge], values.at[frames], halo_send.at[1], halo_recv.at[1], to_beside),
    )
    for halo in halos:
        halo.start()

    def side_copy(index, at, source):
        return remote(source, weight.at[index, 2 * at + side], side_send.at[index, at],
                      weight_recv.at[index, 2 * at + side], to_side)

    def up_copy(index, at, source):
        return remote(source, weight.at[index, 2 * at + side], up_send.at[index, at],
                      weight_recv.at[index, 2 * at + side], to_up)

    def down_copy(index, at, source):
        return remote(source, weight.at[index, 2 * at + side], down_send.at[index, at],
                      weight_recv.at[index, 2 * at + side], to_down)

    for index in range(pieces):
        mine = weight_hbm.at[:, columns(index)]
        side_copy(index, line, mine).start()

        @pl.when(has_up)
        def _():
            up_copy(index, line, mine).start()

        @pl.when(has_down)
        def _():
            down_copy(index, line, mine).start()

        pltpu.make_async_copy(mine, weight.at[index, owner], own_weight.at[index]).start()
    gate_copy = remote(gates.at[group], gates.at[group], gate_send, gate_recv, to_across)

    paired = lines % 2 == 0
    mate = line + 1 - 2 * (line % 2)
    to_mate = {"owner": owner + 2 - 4 * (line % 2)}

    def balanced(index):
        return 2 * index >= pieces if paired else index < 0

    def mate_copy(index):
        source = 2 * line + 1 - side
        block = weight.at[index, source]
        return remote(block, block, mate_send.at[index], weight_recv.at[index, source], to_mate)

    def forward(index, apart):
        below, above = line - apart, line + apart

        @pl.when(below >= 0)
        def _():
            block = weight.at[index, 2 * below + side]
            side_copy(index, below, block).wait_recv()

            @pl.when(has_up)
            def _():
                up_copy(index, below, block).start()

            @pl.when(jnp.logical_not(balanced(index) & (below == mate)))
            def _():
                side_copy(index, below, block).start()

        @pl.when(above < lines)
        def _():
            block = weight.at[index, 2 * above + side]
            side_copy(index, above, block).wait_recv()

            @pl.when(has_down)
            def _():
                down_copy(index, above, block).start()

            @pl.when(jnp.logical_not(balanced(index) & (above == mate)))
            def _():
                side_copy(index, above, block).start()

    def within(index, count):
        return (index >= 0) & (index < count)

    def mate_step(index):
        @pl.when(within(index, pieces) & balanced(index))
        def _():
            mate_copy(index).wait_recv()
            mate_copy(index).start()

    def forward_steps(step):
        for apart in range(lines - 1, 0, -1):
            index = step - LAG * apart

            @pl.when(within(index, pieces))
            def _():
                forward(index, apart)

    def places(ids):
        frame = sum((ids >= spots * step).astype(jnp.int32) for step in range(1, frames + HALO))
        spot = ids - frame * spots
        row = sum((spot >= WB * step).astype(jnp.int32) for step in range(1, spots // WB))
        return frame, row, spot - row * WB

    request = owner // 2
    query_frame, query_row, query_column = places(lax.broadcasted_iota(jnp.int32, (tokens, 1), 0))
    key_at, key_row, key_column = places(lax.broadcasted_iota(jnp.int32, (1, tokens + spots), 1))
    halo_frame = frames - slab
    key_frame = jnp.where(key_at < frames, key_at + slab * frames, halo_frame)
    allowed = jnp.abs(query_frame + slab * frames - key_frame) <= windows_ref[request, 0]
    allowed = allowed & (jnp.abs(query_row - key_row) <= windows_ref[request, 1])
    allowed = allowed & (jnp.abs(query_column - key_column) <= windows_ref[request, 2])
    bias[...] = jnp.where(allowed, 0.0, NEG_LARGE)

    for load in loads:
        load.wait()
    factor = jnp.where(owner % 2 == 1, keep_ref[request], 1).astype(jnp.float32)
    gates[group] = jnp.broadcast_to(gate_own[pl.ds(request, 1), :] * factor, gates.shape[1:])
    for halo in halos:
        halo.wait_recv()

    def rows_copy(batch, origin, send, device):
        block = rows.at[batch, origin]
        return remote(block, block, send, rows_recv.at[batch, origin], device)

    def attend_batch(batch, carry):
        for head in range(span // HEAD_DIM):
            lanes = pl.ds(pl.multiple_of(batch * span + head * HEAD_DIM, HEAD_DIM), HEAD_DIM)
            key_head = keys[:, :, lanes].reshape(-1, HEAD_DIM)
            value_head = values[:, :, lanes].reshape(-1, HEAD_DIM)
            scores = lax.dot_general(
                query[:, lanes], key_head, (((1,), (1,)), ((), ())),
                preferred_element_type=jnp.float32,
            )
            scores = scores * (1.0 / math.sqrt(HEAD_DIM)) + bias[...]
            exponent = jnp.exp(scores - jnp.max(scores, axis=-1, keepdims=True))
            totals = jnp.sum(exponent, axis=-1, keepdims=True)
            mixing = (exponent * (1.0 / totals)).astype(jnp.bfloat16)
            mixture = jnp.dot(mixing, value_head, preferred_element_type=jnp.float32)
            rows[batch, place, :, head * HEAD_DIM:(head + 1) * HEAD_DIM] = mixture.astype(jnp.bfloat16)
        rows_copy(batch, place, rows_send.at[batch, 0], to_across).start()
        rows_copy(batch, place, rows_send.at[batch, 1], to_beside).start()

        mate_step(batch - MATE_LAG)
        relay_step(batch - RELAY_LAG)
        forward_steps(batch)
        return carry

    def relay_step(batch):
        @pl.when(within(batch, batches))
        def _():
            rows_copy(batch, across, relay_send.at[batch], to_beside).wait_recv()
            rows_copy(batch, across, relay_send.at[batch], to_beside).start()

    def forward_round(step, carry):
        mate_step(step - MATE_LAG)
        relay_step(step - RELAY_LAG)
        forward_steps(step)
        return carry

    lax.fori_loop(0, batches, attend_batch, 0)
    gate_copy.start()
    lax.fori_loop(batches, PROJECT_LAG, forward_round, 0)

    def cols_copy(index, slot, device):
        return remote(finished.at[index, slot], out_ref.at[:, columns(index)],
                      cols_send.at[index, slot], cols_recv.at[index, place], device)

    def product(index, whole, receiver, holder):
        total = None
        for batch in range(batches):
            part = jnp.dot(rows[batch, receiver], whole[batch * span:(batch + 1) * span],
                           preferred_element_type=jnp.float32)
            total = part if total is None else total + part
        return (total * gates[holder, :, columns(index)][0:1]).astype(jnp.bfloat16)

    def project(step, carry):
        index = step - PROJECT_LAG
        mate_step(step - MATE_LAG)
        relay_step(step - RELAY_LAG)

        @pl.when(index == 0)
        def _():
            gate_copy.wait_recv()
            for batch in range(batches):
                for origin in (beside, corner):
                    rows_copy(batch, origin, relay_send.at[batch], to_beside).wait_recv()

        pltpu.make_async_copy(weight_hbm.at[:, columns(index)], weight.at[index, owner],
                              own_weight.at[index]).wait()
        for at in range(lines):
            source = 2 * at + 1 - side
            block = weight.at[index, source]

            @pl.when(jnp.logical_not(balanced(index) & (at == line)))
            def _():
                remote(block, block, side_send.at[index, at], weight_recv.at[index, source], to_side).wait_recv()

        whole = weight[index].reshape(owners * depth, PIECE)
        remotes = ((across, 1 - group, to_across), (corner, 1 - group, to_corner), (beside, group, to_beside))
        for slot, (receiver, holder, device) in enumerate(remotes):
            finished[index, slot] = product(index, whole, receiver, holder)
            cols_copy(index, slot, device).start()
        finished[index, 3] = product(index, whole, place, group)
        pltpu.make_async_copy(finished.at[index, 3], out_ref.at[:, columns(index)], own_out.at[index]).start()
        forward_steps(step)
        return carry

    lax.fori_loop(PROJECT_LAG, PROJECT_LAG + pieces, project, 0)

    def drain(index, carry):
        for at in range(lines):
            block = weight.at[index, 2 * at + side]

            @pl.when(jnp.logical_not(balanced(index) & (at == mate)))
            def _():
                side_copy(index, at, block).wait_send()

            @pl.when(has_up & (at <= line))
            def _():
                up_copy(index, at, block).wait_send()

            @pl.when(has_down & (at >= line))
            def _():
                down_copy(index, at, block).wait_send()

        @pl.when(balanced(index))
        def _():
            mate_copy(index).wait_send()

        return carry

    def collect(index, carry):
        pltpu.make_async_copy(finished.at[index, 3], out_ref.at[:, columns(index)], own_out.at[index]).wait()
        for slot, device in enumerate((to_across, to_corner, to_beside)):
            cols_copy(index, slot, device).wait_send()
        for origin in (across, corner, beside):
            remote(finished.at[index, 0], out_ref.at[:, columns(index)], cols_send.at[index, 0],
                   cols_recv.at[index, origin], to_across).wait_recv()
        return carry

    lax.fori_loop(0, pieces, drain, 0)
    for halo in halos:
        halo.wait_send()
    gate_copy.wait_send()
    for batch in range(batches):
        rows_copy(batch, place, rows_send.at[batch, 0], to_across).wait_send()
        rows_copy(batch, place, rows_send.at[batch, 1], to_beside).wait_send()
        rows_copy(batch, across, relay_send.at[batch], to_beside).wait_send()
    lax.fori_loop(0, pieces, collect, 0)


def fused(queries, key_value, keep, windows, gate, out_weight):
    frames, spots, features = queries.shape[1:]
    model_width = gate.shape[1]
    owners = lax.axis_size("owner")
    tokens = frames * spots
    depth = out_weight.shape[0]
    pieces = model_width // 4 // PIECE
    span = HEAD_GROUP * HEAD_DIM
    batches = features // span
    lines = owners // 2
    bf16 = jnp.bfloat16
    dma = pltpu.SemaphoreType.DMA
    whole = pl.BlockSpec(memory_space=pl.ANY)
    result = pl.pallas_call(
        fused_kernel,
        out_shape=pltpu.VMEM((tokens, model_width), bf16),
        in_specs=[whole] * 4 + [pl.BlockSpec(memory_space=pltpu.SMEM)] * 2,
        out_specs=whole,
        scratch_shapes=[
            pltpu.VMEM((tokens, features), bf16),
            pltpu.VMEM((frames + HALO, spots, features), bf16),
            pltpu.VMEM((frames + HALO, spots, features), bf16),
            pltpu.VMEM((pieces, owners, depth, PIECE), bf16),
            pltpu.VMEM((batches, 4, tokens, span), bf16),
            pltpu.VMEM((pieces, 4, tokens, PIECE), bf16),
            pltpu.VMEM((2, 8, model_width), jnp.float32),
            pltpu.VMEM(gate.shape, jnp.float32),
            pltpu.VMEM((tokens, tokens + spots), jnp.float32),
            dma((4,)), dma((2,)), dma((2,)), dma, dma, dma((pieces,)),
            dma((pieces, owners)), dma((pieces, lines)), dma((pieces, lines)), dma((pieces, lines)), dma((pieces,)),
            dma((batches, 4)), dma((batches, 2)), dma((batches,)),
            dma((pieces, 4)), dma((pieces, 3)), dma((pieces,)),
        ],
        compiler_params=pltpu.CompilerParams(
            collective_id=0, has_side_effects=True, vmem_limit_bytes=56 * 2**20,
        ),
    )(
        queries.reshape(tokens, features), key_value.reshape(2, frames, spots, features),
        out_weight, gate, keep, windows,
    )
    return result.reshape(1, frames, spots, model_width)


def on_device(queries, key_value, keep, windows, gate, out_weight):
    frames, spots, features = queries.shape[1:]
    fits = (
        lax.axis_size("slab") == 2
        and lax.axis_size("groups") == 2
        and lax.axis_size("owner") % 2 == 0
        and out_weight.shape[0] % 16 == 0
        and spots % 16 == 0
        and spots % WB == 0
        and features % (HEAD_GROUP * HEAD_DIM) == 0
        and gate.shape[1] % (4 * PIECE) == 0
    )
    chosen = fused if fits else plain
    return chosen(queries, key_value, keep, windows, gate, out_weight)


def solution(mesh):
    placed = (
        P(("groups", "owner"), "slab", None, None),
        P(None, ("groups", "owner"), "slab", None, None),
        P("groups"),
        P("groups", None),
        P("groups", None),
        P("owner", None),
    )
    return jax.shard_map(
        on_device,
        mesh=mesh,
        in_specs=placed,
        out_specs=P(("groups", "owner"), "slab", None, None),
        check_vma=False,
    )
```

```python
import math

import jax
import jax.numpy as jnp
from jax import lax
from jax.experimental import pallas as pl
from jax.experimental.pallas import tpu as pltpu
from jax.sharding import PartitionSpec as P

HEADS = 20
HEAD_DIM = 128
WB = 14
HALO = 1


NEG_LARGE = -1e30
PIECE = 128
HEAD_GROUP = 4
LAG = 2
MATE_LAG = 6
RELAY_LAG = 4
PROJECT_LAG = 8


def padded_2(cells, sides, width):
    for axis, dim in sides:
        count = lax.axis_size(axis)
        ends = count - 1
        head = lax.slice_in_dim(cells, 0, width, axis=dim)
        tail = lax.slice_in_dim(cells, cells.shape[dim] - width, cells.shape[dim], axis=dim)
        cells = jnp.concatenate(
            [
                lax.ppermute(tail, axis, [(i, (i + 1) % count) for i in range(ends)]),
                cells,
                lax.ppermute(head, axis, [((i + 1) % count, i) for i in range(ends)]),
            ],
            axis=dim,
        )
    return cells


def window_mask(window, slab_index, frames_here, frames_total, spots):
    query_ids = jnp.arange(frames_here * spots, dtype=jnp.int32)
    key_ids = jnp.arange((frames_here + 2 * HALO) * spots, dtype=jnp.int32)
    query_frame = slab_index * frames_here + query_ids // spots
    key_frame = slab_index * frames_here - HALO + key_ids // spots
    query_row = query_ids % spots // WB
    key_row = key_ids % spots // WB
    query_column = query_ids % spots % WB
    key_column = key_ids % spots % WB
    inside = (key_frame >= 0) & (key_frame < frames_total)
    allowed = jnp.abs(query_frame[:, None] - key_frame[None, :]) <= window[0]
    allowed = allowed & (jnp.abs(query_row[:, None] - key_row[None, :]) <= window[1])
    allowed = allowed & (jnp.abs(query_column[:, None] - key_column[None, :]) <= window[2])
    return allowed & inside[None, :]


def attend(query_rows, key_rows, value_rows, allowed):
    query_count = query_rows.shape[0]
    key_count = key_rows.shape[0]
    query_heads = query_rows.reshape(query_count, HEADS, HEAD_DIM)
    key_heads = key_rows.reshape(key_count, HEADS, HEAD_DIM)
    value_heads = value_rows.reshape(key_count, HEADS, HEAD_DIM)
    scores = jnp.einsum("qhd,khd->hqk", query_heads, key_heads, preferred_element_type=jnp.float32)
    scores = scores * (1.0 / math.sqrt(HEAD_DIM))
    scores = jnp.where(allowed[None], scores, NEG_LARGE)
    highest = jnp.max(scores, axis=-1, keepdims=True)
    exponent = jnp.exp(scores - highest)
    totals = jnp.sum(exponent, axis=-1, keepdims=True)
    weights = (exponent / totals).astype(jnp.bfloat16)
    mixture = jnp.einsum("hqk,khd->qhd", weights, value_heads, preferred_element_type=jnp.float32)
    return mixture.astype(jnp.bfloat16).reshape(query_count, HEADS * HEAD_DIM)


def plain(queries, key_value, keep, windows, gate, out_weight):
    frames_here = queries.shape[1]
    spots = queries.shape[2]
    features = queries.shape[3]
    model_width = gate.shape[1]
    slab_index = lax.axis_index("slab")
    stream_index = lax.axis_index("owner")
    request = stream_index // 2
    branch = stream_index % 2
    frames_total = frames_here * lax.axis_size("slab")
    window = lax.dynamic_index_in_dim(windows, request, 0, keepdims=False)
    gate_row = lax.dynamic_index_in_dim(gate, request, 0, keepdims=False)
    keep_flag = lax.dynamic_index_in_dim(keep, request, 0, keepdims=False)
    factor = jnp.where(branch == 1, keep_flag, 1)
    padded = padded_2(key_value, (("slab", 2),), HALO)
    allowed = window_mask(window, slab_index, frames_here, frames_total, spots)
    branch_rows = frames_here * spots
    query_rows = queries[0].reshape(branch_rows, features)
    key_rows = padded[0, 0].reshape(-1, features)
    value_rows = padded[1, 0].reshape(-1, features)
    operands = (query_rows, key_rows, value_rows)
    attended_rows = attend(operands[0], operands[1], operands[2], allowed)
    quad = ("groups", "slab")
    parts = lax.axis_size("groups") * lax.axis_size("slab")
    place = lax.axis_index("groups") * lax.axis_size("slab") + slab_index
    width = model_width // parts
    own_columns = lax.dynamic_slice_in_dim(out_weight, place * width, width, 1)
    weight_part = lax.all_gather(own_columns, "owner", axis=0, tiled=True)
    all_rows = lax.all_gather(attended_rows, quad, axis=0, tiled=True)
    scaled_gate = gate_row * factor.astype(jnp.float32)
    gates = lax.all_to_all(
        jnp.broadcast_to(scaled_gate.reshape(parts, 1, width), (parts, 8, width)),
        quad, split_axis=0, concat_axis=0, tiled=True,
    )
    product = jnp.dot(all_rows, weight_part, preferred_element_type=jnp.float32)
    product = product.reshape(parts, branch_rows, width) * gates[:, :1]
    scaled = product.astype(jnp.bfloat16).reshape(parts * branch_rows, width)
    result = lax.all_to_all(scaled, quad, split_axis=0, concat_axis=1, tiled=True)
    return result.reshape((1, frames_here, spots, model_width))


def fused_kernel(
    query_hbm, kv_hbm, weight_hbm, gate_hbm, keep_ref, windows_ref, out_ref,
    query, keys, values, weight, rows, finished, gates, gate_own, bias,
    load_sems, halo_send, halo_recv, gate_send, gate_recv, own_weight,
    weight_recv, side_send, up_send, down_send, mate_send,
    rows_recv, rows_send, relay_send, cols_recv, cols_send, own_out,
):
    group = lax.axis_index("groups")
    owner = lax.axis_index("owner")
    slab = lax.axis_index("slab")
    line, side = owner // 2, owner % 2
    lines = lax.axis_size("owner") // 2
    frames, spots, features = keys.shape[0] - HALO, keys.shape[1], keys.shape[2]
    tokens = frames * spots
    pieces, owners, depth, _ = weight.shape
    batches = rows.shape[0]
    span = features // batches
    quarter = pieces * PIECE
    place = group * 2 + slab
    across = (1 - group) * 2 + slab
    beside = group * 2 + 1 - slab
    corner = (1 - group) * 2 + 1 - slab
    to_side = {"owner": owner + 1 - 2 * side}
    to_up = {"owner": owner + 2}
    to_down = {"owner": owner - 2}
    to_across = {"groups": 1 - group}
    to_beside = {"slab": 1 - slab}
    to_corner = {"groups": 1 - group, "slab": 1 - slab}
    has_up = line + 1 < lines
    has_down = line > 0

    def remote(source, target, send, recv, device):
        return pltpu.make_async_remote_copy(
            src_ref=source, dst_ref=target, send_sem=send, recv_sem=recv,
            device_id=device, device_id_type=pl.DeviceIdType.MESH,
        )

    barrier = pltpu.get_barrier_semaphore()
    for device in (to_side, to_across, to_beside, to_corner):
        pl.semaphore_signal(barrier, inc=1, device_id=device, device_id_type=pl.DeviceIdType.MESH)

    @pl.when(has_up)
    def _():
        pl.semaphore_signal(barrier, inc=1, device_id=to_up, device_id_type=pl.DeviceIdType.MESH)

    @pl.when(has_down)
    def _():
        pl.semaphore_signal(barrier, inc=1, device_id=to_down, device_id_type=pl.DeviceIdType.MESH)

    loads = (
        pltpu.make_async_copy(query_hbm, query, load_sems.at[0]),
        pltpu.make_async_copy(kv_hbm.at[0], keys.at[pl.ds(0, frames)], load_sems.at[1]),
        pltpu.make_async_copy(kv_hbm.at[1], values.at[pl.ds(0, frames)], load_sems.at[2]),
        pltpu.make_async_copy(gate_hbm, gate_own, load_sems.at[3]),
    )
    for load in loads:
        load.start()
    pl.semaphore_wait(barrier, 4 + has_up.astype(jnp.int32) + has_down.astype(jnp.int32))

    def columns(index):
        return pl.ds(pl.multiple_of(place * quarter + index * PIECE, PIECE), PIECE)

    edge = (1 - slab) * (frames - 1)
    halos = (
        remote(kv_hbm.at[0, edge], keys.at[frames], halo_send.at[0], halo_recv.at[0], to_beside),
        remote(kv_hbm.at[1, edge], values.at[frames], halo_send.at[1], halo_recv.at[1], to_beside),
    )
    for halo in halos:
        halo.start()

    def side_copy(index, at, source):
        return remote(source, weight.at[index, 2 * at + side], side_send.at[index, at],
                      weight_recv.at[index, 2 * at + side], to_side)

    def up_copy(index, at, source):
        return remote(source, weight.at[index, 2 * at + side], up_send.at[index, at],
                      weight_recv.at[index, 2 * at + side], to_up)

    def down_copy(index, at, source):
        return remote(source, weight.at[index, 2 * at + side], down_send.at[index, at],
                      weight_recv.at[index, 2 * at + side], to_down)

    for index in range(pieces):
        mine = weight_hbm.at[:, columns(index)]
        side_copy(index, line, mine).start()

        @pl.when(has_up)
        def _():
            up_copy(index, line, mine).start()

        @pl.when(has_down)
        def _():
            down_copy(index, line, mine).start()

        pltpu.make_async_copy(mine, weight.at[index, owner], own_weight.at[index]).start()
    gate_copy = remote(gates.at[group], gates.at[group], gate_send, gate_recv, to_across)

    paired = lines % 2 == 0
    mate = line + 1 - 2 * (line % 2)
    to_mate = {"owner": owner + 2 - 4 * (line % 2)}

    def balanced(index):
        return 2 * index >= pieces if paired else index < 0

    def mate_copy(index):
        source = 2 * line + 1 - side
        block = weight.at[index, source]
        return remote(block, block, mate_send.at[index], weight_recv.at[index, source], to_mate)

    def forward(index, apart):
        below, above = line - apart, line + apart

        @pl.when(below >= 0)
        def _():
            block = weight.at[index, 2 * below + side]
            side_copy(index, below, block).wait_recv()

            @pl.when(has_up)
            def _():
                up_copy(index, below, block).start()

            @pl.when(jnp.logical_not(balanced(index) & (below == mate)))
            def _():
                side_copy(index, below, block).start()

        @pl.when(above < lines)
        def _():
            block = weight.at[index, 2 * above + side]
            side_copy(index, above, block).wait_recv()

            @pl.when(has_down)
            def _():
                down_copy(index, above, block).start()

            @pl.when(jnp.logical_not(balanced(index) & (above == mate)))
            def _():
                side_copy(index, above, block).start()

    def within(index, count):
        return (index >= 0) & (index < count)

    def mate_step(index):
        @pl.when(within(index, pieces) & balanced(index))
        def _():
            mate_copy(index).wait_recv()
            mate_copy(index).start()

    def forward_steps(step, first=0, last=0):
        for apart in range(last or lines - 1, first, -1):
            index = step - LAG * apart

            @pl.when(within(index, pieces))
            def _():
                forward(index, apart)

    def places(ids):
        frame = sum((ids >= spots * step).astype(jnp.int32) for step in range(1, frames + HALO))
        spot = ids - frame * spots
        row = sum((spot >= WB * step).astype(jnp.int32) for step in range(1, spots // WB))
        return frame, row, spot - row * WB

    request = owner // 2
    query_frame, query_row, query_column = places(lax.broadcasted_iota(jnp.int32, (tokens, 1), 0))
    key_at, key_row, key_column = places(lax.broadcasted_iota(jnp.int32, (1, tokens + spots), 1))
    halo_frame = frames - slab
    key_frame = jnp.where(key_at < frames, key_at + slab * frames, halo_frame)
    allowed = jnp.abs(query_frame + slab * frames - key_frame) <= windows_ref[request, 0]
    allowed = allowed & (jnp.abs(query_row - key_row) <= windows_ref[request, 1])
    allowed = allowed & (jnp.abs(query_column - key_column) <= windows_ref[request, 2])
    bias[...] = jnp.where(allowed, 0.0, NEG_LARGE)

    for load in loads:
        load.wait()
    factor = jnp.where(owner % 2 == 1, keep_ref[request], 1).astype(jnp.float32)
    gates[group] = jnp.broadcast_to(gate_own[pl.ds(request, 1), :] * factor, gates.shape[1:])
    for halo in halos:
        halo.wait_recv()

    def rows_copy(batch, origin, send, device):
        block = rows.at[batch, origin]
        return remote(block, block, send, rows_recv.at[batch, origin], device)

    def attend_batch(batch, carry):
        for head in range(span // HEAD_DIM):
            lanes = pl.ds(pl.multiple_of(batch * span + head * HEAD_DIM, HEAD_DIM), HEAD_DIM)
            key_head = keys[:, :, lanes].reshape(-1, HEAD_DIM)
            value_head = values[:, :, lanes].reshape(-1, HEAD_DIM)
            scores = lax.dot_general(
                query[:, lanes], key_head, (((1,), (1,)), ((), ())),
                preferred_element_type=jnp.float32,
            )
            scores = scores * (1.0 / math.sqrt(HEAD_DIM)) + bias[...]
            exponent = jnp.exp(scores - jnp.max(scores, axis=-1, keepdims=True))
            totals = jnp.sum(exponent, axis=-1, keepdims=True)
            mixing = (exponent * (1.0 / totals)).astype(jnp.bfloat16)
            mixture = jnp.dot(mixing, value_head, preferred_element_type=jnp.float32)
            rows[batch, place, :, head * HEAD_DIM:(head + 1) * HEAD_DIM] = mixture.astype(jnp.bfloat16)
        rows_copy(batch, place, rows_send.at[batch, 0], to_across).start()
        rows_copy(batch, place, rows_send.at[batch, 1], to_beside).start()

        mate_step(batch - MATE_LAG)
        relay_step(batch - RELAY_LAG)
        forward_steps(batch)
        return carry

    def relay_step(batch):
        @pl.when(within(batch, batches))
        def _():
            rows_copy(batch, across, relay_send.at[batch], to_beside).wait_recv()
            rows_copy(batch, across, relay_send.at[batch], to_beside).start()

    def forward_round(step, carry):
        mate_step(step - MATE_LAG)
        relay_step(step - RELAY_LAG)
        forward_steps(step)
        return carry

    lax.fori_loop(0, batches, attend_batch, 0)
    gate_copy.start()
    lax.fori_loop(batches, PROJECT_LAG, forward_round, 0)

    def cols_copy(index, slot, device):
        return remote(finished.at[index, slot], out_ref.at[:, columns(index)],
                      cols_send.at[index, slot], cols_recv.at[index, place], device)

    def product(index, whole, receiver, holder):
        total = None
        for batch in range(batches):
            part = jnp.dot(rows[batch, receiver], whole[batch * span:(batch + 1) * span],
                           preferred_element_type=jnp.float32)
            total = part if total is None else total + part
        return (total * gates[holder, :, columns(index)][0:1]).astype(jnp.bfloat16)

    def project(step, carry):
        index = step - PROJECT_LAG
        mate_step(step - MATE_LAG)
        relay_step(step - RELAY_LAG)

        @pl.when(index == 0)
        def _():
            gate_copy.wait_recv()
            for batch in range(batches):
                for origin in (beside, corner):
                    rows_copy(batch, origin, relay_send.at[batch], to_beside).wait_recv()

        pltpu.make_async_copy(weight_hbm.at[:, columns(index)], weight.at[index, owner],
                              own_weight.at[index]).wait()
        for at in range(lines):
            source = 2 * at + 1 - side
            block = weight.at[index, source]

            @pl.when(jnp.logical_not(balanced(index) & (at == line)))
            def _():
                remote(block, block, side_send.at[index, at], weight_recv.at[index, source], to_side).wait_recv()

        whole = weight[index].reshape(owners * depth, PIECE)
        remotes = ((across, 1 - group, to_across), (corner, 1 - group, to_corner), (beside, group, to_beside))
        for slot, (receiver, holder, device) in enumerate(remotes):
            finished[index, slot] = product(index, whole, receiver, holder)
            cols_copy(index, slot, device).start()
            if slot == 0:
                forward_steps(step, 1)
            elif slot == 1:
                forward_steps(step, 0, 1)
        finished[index, 3] = product(index, whole, place, group)
        pltpu.make_async_copy(finished.at[index, 3], out_ref.at[:, columns(index)], own_out.at[index]).start()
        return carry

    lax.fori_loop(PROJECT_LAG, PROJECT_LAG + pieces, project, 0)

    def drain(index, carry):
        for at in range(lines):
            block = weight.at[index, 2 * at + side]

            @pl.when(jnp.logical_not(balanced(index) & (at == mate)))
            def _():
                side_copy(index, at, block).wait_send()

            @pl.when(has_up & (at <= line))
            def _():
                up_copy(index, at, block).wait_send()

            @pl.when(has_down & (at >= line))
            def _():
                down_copy(index, at, block).wait_send()

        @pl.when(balanced(index))
        def _():
            mate_copy(index).wait_send()

        return carry

    def collect(index, carry):
        pltpu.make_async_copy(finished.at[index, 3], out_ref.at[:, columns(index)], own_out.at[index]).wait()
        for slot, device in enumerate((to_across, to_corner, to_beside)):
            cols_copy(index, slot, device).wait_send()
        for origin in (across, corner, beside):
            remote(finished.at[index, 0], out_ref.at[:, columns(index)], cols_send.at[index, 0],
                   cols_recv.at[index, origin], to_across).wait_recv()
        return carry

    lax.fori_loop(0, pieces, drain, 0)
    for halo in halos:
        halo.wait_send()
    gate_copy.wait_send()
    for batch in range(batches):
        rows_copy(batch, place, rows_send.at[batch, 0], to_across).wait_send()
        rows_copy(batch, place, rows_send.at[batch, 1], to_beside).wait_send()
        rows_copy(batch, across, relay_send.at[batch], to_beside).wait_send()
    lax.fori_loop(0, pieces, collect, 0)


def fused(queries, key_value, keep, windows, gate, out_weight):
    frames, spots, features = queries.shape[1:]
    model_width = gate.shape[1]
    owners = lax.axis_size("owner")
    tokens = frames * spots
    depth = out_weight.shape[0]
    pieces = model_width // 4 // PIECE
    span = HEAD_GROUP * HEAD_DIM
    batches = features // span
    lines = owners // 2
    bf16 = jnp.bfloat16
    dma = pltpu.SemaphoreType.DMA
    whole = pl.BlockSpec(memory_space=pl.ANY)
    result = pl.pallas_call(
        fused_kernel,
        out_shape=pltpu.VMEM((tokens, model_width), bf16),
        in_specs=[whole] * 4 + [pl.BlockSpec(memory_space=pltpu.SMEM)] * 2,
        out_specs=whole,
        scratch_shapes=[
            pltpu.VMEM((tokens, features), bf16),
            pltpu.VMEM((frames + HALO, spots, features), bf16),
            pltpu.VMEM((frames + HALO, spots, features), bf16),
            pltpu.VMEM((pieces, owners, depth, PIECE), bf16),
            pltpu.VMEM((batches, 4, tokens, span), bf16),
            pltpu.VMEM((pieces, 4, tokens, PIECE), bf16),
            pltpu.VMEM((2, 8, model_width), jnp.float32),
            pltpu.VMEM(gate.shape, jnp.float32),
            pltpu.VMEM((tokens, tokens + spots), jnp.float32),
            dma((4,)), dma((2,)), dma((2,)), dma, dma, dma((pieces,)),
            dma((pieces, owners)), dma((pieces, lines)), dma((pieces, lines)), dma((pieces, lines)), dma((pieces,)),
            dma((batches, 4)), dma((batches, 2)), dma((batches,)),
            dma((pieces, 4)), dma((pieces, 3)), dma((pieces,)),
        ],
        compiler_params=pltpu.CompilerParams(
            collective_id=0, has_side_effects=True, vmem_limit_bytes=56 * 2**20,
        ),
    )(
        queries.reshape(tokens, features), key_value.reshape(2, frames, spots, features),
        out_weight, gate, keep, windows,
    )
    return result.reshape(1, frames, spots, model_width)


def on_device(queries, key_value, keep, windows, gate, out_weight):
    frames, spots, features = queries.shape[1:]
    fits = (
        lax.axis_size("slab") == 2
        and lax.axis_size("groups") == 2
        and lax.axis_size("owner") % 2 == 0
        and out_weight.shape[0] % 16 == 0
        and spots % 16 == 0
        and spots % WB == 0
        and features % (HEAD_GROUP * HEAD_DIM) == 0
        and gate.shape[1] % (4 * PIECE) == 0
    )
    chosen = fused if fits else plain
    return chosen(queries, key_value, keep, windows, gate, out_weight)


def solution(mesh):
    placed = (
        P(("groups", "owner"), "slab", None, None),
        P(None, ("groups", "owner"), "slab", None, None),
        P("groups"),
        P("groups", None),
        P("groups", None),
        P("owner", None),
    )
    return jax.shard_map(
        on_device,
        mesh=mesh,
        in_specs=placed,
        out_specs=P(("groups", "owner"), "slab", None, None),
        check_vma=False,
    )
```

```python
import math

import jax
import jax.numpy as jnp
from jax import lax
from jax.experimental import pallas as pl
from jax.experimental.pallas import tpu as pltpu
from jax.sharding import PartitionSpec as P

HEADS = 20
HEAD_DIM = 128
WB = 14
HALO = 1


NEG_LARGE = -1e30
PIECE = 128
HEAD_GROUP = 4
LAG = 2
MATE_LAG = 6
RELAY_LAG = 4
PROJECT_LAG = 8


def padded_2(cells, sides, width):
    for axis, dim in sides:
        count = lax.axis_size(axis)
        ends = count - 1
        head = lax.slice_in_dim(cells, 0, width, axis=dim)
        tail = lax.slice_in_dim(cells, cells.shape[dim] - width, cells.shape[dim], axis=dim)
        cells = jnp.concatenate(
            [
                lax.ppermute(tail, axis, [(i, (i + 1) % count) for i in range(ends)]),
                cells,
                lax.ppermute(head, axis, [((i + 1) % count, i) for i in range(ends)]),
            ],
            axis=dim,
        )
    return cells


def window_mask(window, slab_index, frames_here, frames_total, spots):
    query_ids = jnp.arange(frames_here * spots, dtype=jnp.int32)
    key_ids = jnp.arange((frames_here + 2 * HALO) * spots, dtype=jnp.int32)
    query_frame = slab_index * frames_here + query_ids // spots
    key_frame = slab_index * frames_here - HALO + key_ids // spots
    query_row = query_ids % spots // WB
    key_row = key_ids % spots // WB
    query_column = query_ids % spots % WB
    key_column = key_ids % spots % WB
    inside = (key_frame >= 0) & (key_frame < frames_total)
    allowed = jnp.abs(query_frame[:, None] - key_frame[None, :]) <= window[0]
    allowed = allowed & (jnp.abs(query_row[:, None] - key_row[None, :]) <= window[1])
    allowed = allowed & (jnp.abs(query_column[:, None] - key_column[None, :]) <= window[2])
    return allowed & inside[None, :]


def attend(query_rows, key_rows, value_rows, allowed):
    query_count = query_rows.shape[0]
    key_count = key_rows.shape[0]
    query_heads = query_rows.reshape(query_count, HEADS, HEAD_DIM)
    key_heads = key_rows.reshape(key_count, HEADS, HEAD_DIM)
    value_heads = value_rows.reshape(key_count, HEADS, HEAD_DIM)
    scores = jnp.einsum("qhd,khd->hqk", query_heads, key_heads, preferred_element_type=jnp.float32)
    scores = scores * (1.0 / math.sqrt(HEAD_DIM))
    scores = jnp.where(allowed[None], scores, NEG_LARGE)
    highest = jnp.max(scores, axis=-1, keepdims=True)
    exponent = jnp.exp(scores - highest)
    totals = jnp.sum(exponent, axis=-1, keepdims=True)
    weights = (exponent / totals).astype(jnp.bfloat16)
    mixture = jnp.einsum("hqk,khd->qhd", weights, value_heads, preferred_element_type=jnp.float32)
    return mixture.astype(jnp.bfloat16).reshape(query_count, HEADS * HEAD_DIM)


def plain(queries, key_value, keep, windows, gate, out_weight):
    frames_here = queries.shape[1]
    spots = queries.shape[2]
    features = queries.shape[3]
    model_width = gate.shape[1]
    slab_index = lax.axis_index("slab")
    stream_index = lax.axis_index("owner")
    request = stream_index // 2
    branch = stream_index % 2
    frames_total = frames_here * lax.axis_size("slab")
    window = lax.dynamic_index_in_dim(windows, request, 0, keepdims=False)
    gate_row = lax.dynamic_index_in_dim(gate, request, 0, keepdims=False)
    keep_flag = lax.dynamic_index_in_dim(keep, request, 0, keepdims=False)
    factor = jnp.where(branch == 1, keep_flag, 1)
    padded = padded_2(key_value, (("slab", 2),), HALO)
    allowed = window_mask(window, slab_index, frames_here, frames_total, spots)
    branch_rows = frames_here * spots
    query_rows = queries[0].reshape(branch_rows, features)
    key_rows = padded[0, 0].reshape(-1, features)
    value_rows = padded[1, 0].reshape(-1, features)
    operands = (query_rows, key_rows, value_rows)
    attended_rows = attend(operands[0], operands[1], operands[2], allowed)
    quad = ("groups", "slab")
    parts = lax.axis_size("groups") * lax.axis_size("slab")
    place = lax.axis_index("groups") * lax.axis_size("slab") + slab_index
    width = model_width // parts
    own_columns = lax.dynamic_slice_in_dim(out_weight, place * width, width, 1)
    weight_part = lax.all_gather(own_columns, "owner", axis=0, tiled=True)
    all_rows = lax.all_gather(attended_rows, quad, axis=0, tiled=True)
    scaled_gate = gate_row * factor.astype(jnp.float32)
    gates = lax.all_to_all(
        jnp.broadcast_to(scaled_gate.reshape(parts, 1, width), (parts, 8, width)),
        quad, split_axis=0, concat_axis=0, tiled=True,
    )
    product = jnp.dot(all_rows, weight_part, preferred_element_type=jnp.float32)
    product = product.reshape(parts, branch_rows, width) * gates[:, :1]
    scaled = product.astype(jnp.bfloat16).reshape(parts * branch_rows, width)
    result = lax.all_to_all(scaled, quad, split_axis=0, concat_axis=1, tiled=True)
    return result.reshape((1, frames_here, spots, model_width))


def fused_kernel(
    query_hbm, kv_hbm, weight_hbm, gate_hbm, keep_ref, windows_ref, out_ref,
    query, keys, values, weight, rows, finished, gates, gate_own, bias,
    load_sems, halo_send, halo_recv, gate_send, gate_recv, own_weight,
    z_recv, near_recv, far_recv, side_send, up_send, down_send, mate_send,
    rows_recv, pair_recv, rows_send, cols_recv, cols_send, own_out,
):
    group = lax.axis_index("groups")
    owner = lax.axis_index("owner")
    slab = lax.axis_index("slab")
    line, side = owner // 2, owner % 2
    lines = lax.axis_size("owner") // 2
    frames, spots, features = keys.shape[0] - HALO, keys.shape[1], keys.shape[2]
    tokens = frames * spots
    pieces, owners, depth, _ = weight.shape
    batches = rows.shape[0]
    span = features // batches
    quarter = pieces * PIECE
    place = group * 2 + slab
    across = (1 - group) * 2 + slab
    beside = group * 2 + 1 - slab
    corner = (1 - group) * 2 + 1 - slab
    to_side = {"owner": owner + 1 - 2 * side}
    to_up = {"owner": owner + 2}
    to_down = {"owner": owner - 2}
    to_across = {"groups": 1 - group}
    to_beside = {"slab": 1 - slab}
    to_corner = {"groups": 1 - group, "slab": 1 - slab}
    has_up = line + 1 < lines
    has_down = line > 0

    def remote(source, target, send, recv, device):
        return pltpu.make_async_remote_copy(
            src_ref=source, dst_ref=target, send_sem=send, recv_sem=recv,
            device_id=device, device_id_type=pl.DeviceIdType.MESH,
        )

    barrier = pltpu.get_barrier_semaphore()
    for device in (to_side, to_across, to_beside, to_corner):
        pl.semaphore_signal(barrier, inc=1, device_id=device, device_id_type=pl.DeviceIdType.MESH)

    @pl.when(has_up)
    def _():
        pl.semaphore_signal(barrier, inc=1, device_id=to_up, device_id_type=pl.DeviceIdType.MESH)

    @pl.when(has_down)
    def _():
        pl.semaphore_signal(barrier, inc=1, device_id=to_down, device_id_type=pl.DeviceIdType.MESH)

    loads = (
        pltpu.make_async_copy(query_hbm, query, load_sems.at[0]),
        pltpu.make_async_copy(kv_hbm.at[0], keys.at[pl.ds(0, frames)], load_sems.at[1]),
        pltpu.make_async_copy(kv_hbm.at[1], values.at[pl.ds(0, frames)], load_sems.at[2]),
        pltpu.make_async_copy(gate_hbm, gate_own, load_sems.at[3]),
    )
    for load in loads:
        load.start()
    pl.semaphore_wait(barrier, 4 + has_up.astype(jnp.int32) + has_down.astype(jnp.int32))

    def columns(index):
        return pl.ds(pl.multiple_of(place * quarter + index * PIECE, PIECE), PIECE)

    edge = (1 - slab) * (frames - 1)
    halos = (
        remote(kv_hbm.at[0, edge], keys.at[frames], halo_send.at[0], halo_recv.at[0], to_beside),
        remote(kv_hbm.at[1, edge], values.at[frames], halo_send.at[1], halo_recv.at[1], to_beside),
    )
    for halo in halos:
        halo.start()

    def own_copy(index, source):
        return remote(source, weight.at[index, owner], side_send, near_recv.at[index], to_side)

    def side_copy(index, at, source):
        return remote(source, weight.at[index, 2 * at + side], side_send, far_recv.at[index], to_side)

    def up_copy(index, at, source):
        return remote(source, weight.at[index, 2 * at + side], up_send, z_recv.at[index, at], to_up)

    def down_copy(index, at, source):
        return remote(source, weight.at[index, 2 * at + side], down_send, z_recv.at[index, at], to_down)

    for index in range(pieces):
        mine = weight_hbm.at[:, columns(index)]
        own_copy(index, mine).start()

        @pl.when(has_up)
        def _():
            up_copy(index, line, mine).start()

        @pl.when(has_down)
        def _():
            down_copy(index, line, mine).start()

        pltpu.make_async_copy(mine, weight.at[index, owner], own_weight).start()
    gate_copy = remote(gates.at[group], gates.at[group], gate_send, gate_recv, to_across)

    paired = lines % 2 == 0
    mate = line + 1 - 2 * (line % 2)
    to_mate = {"owner": owner + 2 - 4 * (line % 2)}

    def balanced(index):
        return 2 * index >= pieces if paired else index < 0

    def mate_copy(index):
        source = 2 * line + 1 - side
        block = weight.at[index, source]
        return remote(block, block, mate_send, far_recv.at[index], to_mate)

    def forward(index, apart):
        below, above = line - apart, line + apart

        @pl.when(below >= 0)
        def _():
            block = weight.at[index, 2 * below + side]
            up_copy(index, below, block).wait_recv()

            @pl.when(has_up)
            def _():
                up_copy(index, below, block).start()

            @pl.when(jnp.logical_not(balanced(index) & (below == mate)))
            def _():
                side_copy(index, below, block).start()

        @pl.when(above < lines)
        def _():
            block = weight.at[index, 2 * above + side]
            down_copy(index, above, block).wait_recv()

            @pl.when(has_down)
            def _():
                down_copy(index, above, block).start()

            @pl.when(jnp.logical_not(balanced(index) & (above == mate)))
            def _():
                side_copy(index, above, block).start()

    def within(index, count):
        return (index >= 0) & (index < count)

    def near_wait(index):
        block = weight.at[index, 2 * line + 1 - side]
        remote(block, block, side_send, near_recv.at[index], to_side).wait_recv()

    def mate_step(index):
        @pl.when(within(index, pieces) & balanced(index))
        def _():
            near_wait(index)
            mate_copy(index).start()

    def forward_steps(step, first=0, last=0):
        for apart in range(last or lines - 1, first, -1):
            index = step - LAG * apart

            @pl.when(within(index, pieces))
            def _():
                forward(index, apart)

    def places(ids):
        frame = sum((ids >= spots * step).astype(jnp.int32) for step in range(1, frames + HALO))
        spot = ids - frame * spots
        row = sum((spot >= WB * step).astype(jnp.int32) for step in range(1, spots // WB))
        return frame, row, spot - row * WB

    request = owner // 2
    query_frame, query_row, query_column = places(lax.broadcasted_iota(jnp.int32, (tokens, 1), 0))
    key_at, key_row, key_column = places(lax.broadcasted_iota(jnp.int32, (1, tokens + spots), 1))
    halo_frame = frames - slab
    key_frame = jnp.where(key_at < frames, key_at + slab * frames, halo_frame)
    allowed = jnp.abs(query_frame + slab * frames - key_frame) <= windows_ref[request, 0]
    allowed = allowed & (jnp.abs(query_row - key_row) <= windows_ref[request, 1])
    allowed = allowed & (jnp.abs(query_column - key_column) <= windows_ref[request, 2])
    bias[...] = jnp.where(allowed, 0.0, NEG_LARGE)

    for load in loads:
        load.wait()
    factor = jnp.where(owner % 2 == 1, keep_ref[request], 1).astype(jnp.float32)
    gates[group] = jnp.broadcast_to(gate_own[pl.ds(request, 1), :] * factor, gates.shape[1:])
    for halo in halos:
        halo.wait_recv()

    def rows_copy(batch, origin, recv, device):
        block = rows.at[batch, origin]
        return remote(block, block, rows_send, recv, device)

    def attend_batch(batch, carry):
        for head in range(span // HEAD_DIM):
            lanes = pl.ds(pl.multiple_of(batch * span + head * HEAD_DIM, HEAD_DIM), HEAD_DIM)
            key_head = keys[:, :, lanes].reshape(-1, HEAD_DIM)
            value_head = values[:, :, lanes].reshape(-1, HEAD_DIM)
            scores = lax.dot_general(
                query[:, lanes], key_head, (((1,), (1,)), ((), ())),
                preferred_element_type=jnp.float32,
            )
            scores = scores * (1.0 / math.sqrt(HEAD_DIM)) + bias[...]
            exponent = jnp.exp(scores - jnp.max(scores, axis=-1, keepdims=True))
            totals = jnp.sum(exponent, axis=-1, keepdims=True)
            mixing = (exponent * (1.0 / totals)).astype(jnp.bfloat16)
            mixture = jnp.dot(mixing, value_head, preferred_element_type=jnp.float32)
            rows[batch, place, :, head * HEAD_DIM:(head + 1) * HEAD_DIM] = mixture.astype(jnp.bfloat16)
        rows_copy(batch, place, rows_recv.at[batch], to_across).start()
        rows_copy(batch, place, pair_recv.at[0], to_beside).start()

        mate_step(batch - MATE_LAG)
        relay_step(batch - RELAY_LAG)
        forward_steps(batch)
        return carry

    def relay_step(batch):
        @pl.when(within(batch, batches))
        def _():
            rows_copy(batch, across, rows_recv.at[batch], to_across).wait_recv()
            rows_copy(batch, across, pair_recv.at[1], to_beside).start()

    def forward_round(step, carry):
        mate_step(step - MATE_LAG)
        relay_step(step - RELAY_LAG)
        forward_steps(step)
        return carry

    lax.fori_loop(0, batches, attend_batch, 0)
    gate_copy.start()
    lax.fori_loop(batches, PROJECT_LAG, forward_round, 0)

    def cols_copy(index, slot, device):
        return remote(finished.at[index, slot], out_ref.at[:, columns(index)],
                      cols_send, cols_recv.at[place], device)

    def product(index, receiver, holder):
        whole = weight[index].reshape(owners * depth, PIECE)
        total = None
        for batch in range(batches):
            part = jnp.dot(rows[batch, receiver], whole[batch * span:(batch + 1) * span],
                           preferred_element_type=jnp.float32)
            total = part if total is None else total + part
        return (total * gates[holder, :, columns(index)][0:1]).astype(jnp.bfloat16)

    def receive_place(index):
        finished[index, 3] = product(index, place, group)
        pltpu.make_async_copy(finished.at[index, 3], out_ref.at[:, columns(index)], own_out).start()

    def serve(index, slot):
        receiver, holder, device = ((across, 1 - group, to_across), (corner, 1 - group, to_corner), (beside, group, to_beside))[slot]
        finished[index, slot] = product(index, receiver, holder)
        cols_copy(index, slot, device).start()

    def project(step, carry):
        index = step - PROJECT_LAG
        mate_step(step - MATE_LAG)
        relay_step(step - RELAY_LAG)

        @pl.when(index == 0)
        def _():
            gate_copy.wait_recv()
            for at, origin in enumerate((beside, corner)):
                every = rows.at[:, origin]
                remote(every, every, rows_send, pair_recv.at[at], to_beside).wait_recv()
            mine = weight.at[:, owner]
            pltpu.make_async_copy(mine, mine, own_weight).wait()

        @pl.when(jnp.logical_not(balanced(index)))
        def _():
            near_wait(index)

        if lines > 1:
            others = weight.at[index, pl.ds(0, lines - 1)]
            remote(others, others, side_send, far_recv.at[index], to_side).wait_recv()
        serve(index, 0)
        forward_steps(step, 1)
        serve(index, 1)
        forward_steps(step, 0, 1)
        serve(index, 2)

        @pl.when(index > 0)
        def _():
            receive_place(index - 1)

        return carry

    lax.fori_loop(PROJECT_LAG, PROJECT_LAG + pieces, project, 0)
    receive_place(pieces - 1)

    def sent(blocks, send):
        remote(blocks, blocks, send, near_recv.at[0], to_side).wait_send()

    if paired:
        sent(weight.at[pl.ds(0, pieces // 2), pl.ds(0, owners - 1)], side_send)
        sent(weight.at[pl.ds(0, pieces // 2), 0], mate_send)
    else:
        sent(weight.at[:, pl.ds(0, lines)], side_send)
    for at in range(lines):
        if at + 1 < lines:
            @pl.when(line == at)
            def _():
                sent(weight.at[:, pl.ds(0, at + 1)], up_send)
        if at > 0:
            @pl.when(line == at)
            def _():
                sent(weight.at[:, pl.ds(0, lines - at)], down_send)
    for halo in halos:
        halo.wait_send()
    gate_copy.wait_send()
    sent(rows.at[:, pl.ds(0, 3)], rows_send)
    sent(finished.at[:, pl.ds(0, 3)], cols_send)

    def quarter_of(origin):
        return out_ref.at[:, pl.ds(pl.multiple_of(origin * quarter, PIECE), quarter)]

    pltpu.make_async_copy(quarter_of(place), quarter_of(place), own_out).wait()
    for origin in (beside, across, corner):
        remote(quarter_of(origin), quarter_of(origin), cols_send, cols_recv.at[origin], to_across).wait_recv()


def fused(queries, key_value, keep, windows, gate, out_weight):
    frames, spots, features = queries.shape[1:]
    model_width = gate.shape[1]
    owners = lax.axis_size("owner")
    tokens = frames * spots
    depth = out_weight.shape[0]
    pieces = model_width // 4 // PIECE
    span = HEAD_GROUP * HEAD_DIM
    batches = features // span
    lines = owners // 2
    bf16 = jnp.bfloat16
    dma = pltpu.SemaphoreType.DMA
    whole = pl.BlockSpec(memory_space=pl.ANY)
    result = pl.pallas_call(
        fused_kernel,
        out_shape=pltpu.VMEM((tokens, model_width), bf16),
        in_specs=[whole] * 4 + [pl.BlockSpec(memory_space=pltpu.SMEM)] * 2,
        out_specs=whole,
        scratch_shapes=[
            pltpu.VMEM((tokens, features), bf16),
            pltpu.VMEM((frames + HALO, spots, features), bf16),
            pltpu.VMEM((frames + HALO, spots, features), bf16),
            pltpu.VMEM((pieces, owners, depth, PIECE), bf16),
            pltpu.VMEM((batches, 4, tokens, span), bf16),
            pltpu.VMEM((pieces, 4, tokens, PIECE), bf16),
            pltpu.VMEM((2, 8, model_width), jnp.float32),
            pltpu.VMEM(gate.shape, jnp.float32),
            pltpu.VMEM((tokens, tokens + spots), jnp.float32),
            dma((4,)), dma((2,)), dma((2,)), dma, dma, dma,
            dma((pieces, lines)), dma((pieces,)), dma((pieces,)), dma, dma, dma, dma,
            dma((batches,)), dma((2,)), dma,
            dma((4,)), dma, dma,
        ],
        compiler_params=pltpu.CompilerParams(
            collective_id=0, has_side_effects=True, vmem_limit_bytes=56 * 2**20,
        ),
    )(
        queries.reshape(tokens, features), key_value.reshape(2, frames, spots, features),
        out_weight, gate, keep, windows,
    )
    return result.reshape(1, frames, spots, model_width)


def on_device(queries, key_value, keep, windows, gate, out_weight):
    frames, spots, features = queries.shape[1:]
    fits = (
        lax.axis_size("slab") == 2
        and lax.axis_size("groups") == 2
        and lax.axis_size("owner") % 2 == 0
        and out_weight.shape[0] % 16 == 0
        and spots % 16 == 0
        and spots % WB == 0
        and features % (HEAD_GROUP * HEAD_DIM) == 0
        and gate.shape[1] % (8 * PIECE) == 0
    )
    chosen = fused if fits else plain
    return chosen(queries, key_value, keep, windows, gate, out_weight)


def solution(mesh):
    placed = (
        P(("groups", "owner"), "slab", None, None),
        P(None, ("groups", "owner"), "slab", None, None),
        P("groups"),
        P("groups", None),
        P("groups", None),
        P("owner", None),
    )
    return jax.shard_map(
        on_device,
        mesh=mesh,
        in_specs=placed,
        out_specs=P(("groups", "owner"), "slab", None, None),
        check_vma=False,
    )
```

```python
import math

import jax
import jax.numpy as jnp
from jax import lax
from jax.experimental import pallas as pl
from jax.experimental.pallas import tpu as pltpu
from jax.sharding import PartitionSpec as P

HEADS = 20
HEAD_DIM = 128
WB = 14
HALO = 1


NEG_LARGE = -1e30
PIECE = 128
HEAD_GROUP = 4
LAG = 2
MATE_LAG = 6
RELAY_LAG = 4
PROJECT_LAG = 8


def padded_2(cells, sides, width):
    for axis, dim in sides:
        count = lax.axis_size(axis)
        ends = count - 1
        head = lax.slice_in_dim(cells, 0, width, axis=dim)
        tail = lax.slice_in_dim(cells, cells.shape[dim] - width, cells.shape[dim], axis=dim)
        cells = jnp.concatenate(
            [
                lax.ppermute(tail, axis, [(i, (i + 1) % count) for i in range(ends)]),
                cells,
                lax.ppermute(head, axis, [((i + 1) % count, i) for i in range(ends)]),
            ],
            axis=dim,
        )
    return cells


def window_mask(window, slab_index, frames_here, frames_total, spots):
    query_ids = jnp.arange(frames_here * spots, dtype=jnp.int32)
    key_ids = jnp.arange((frames_here + 2 * HALO) * spots, dtype=jnp.int32)
    query_frame = slab_index * frames_here + query_ids // spots
    key_frame = slab_index * frames_here - HALO + key_ids // spots
    query_row = query_ids % spots // WB
    key_row = key_ids % spots // WB
    query_column = query_ids % spots % WB
    key_column = key_ids % spots % WB
    inside = (key_frame >= 0) & (key_frame < frames_total)
    allowed = jnp.abs(query_frame[:, None] - key_frame[None, :]) <= window[0]
    allowed = allowed & (jnp.abs(query_row[:, None] - key_row[None, :]) <= window[1])
    allowed = allowed & (jnp.abs(query_column[:, None] - key_column[None, :]) <= window[2])
    return allowed & inside[None, :]


def attend(query_rows, key_rows, value_rows, allowed):
    query_count = query_rows.shape[0]
    key_count = key_rows.shape[0]
    query_heads = query_rows.reshape(query_count, HEADS, HEAD_DIM)
    key_heads = key_rows.reshape(key_count, HEADS, HEAD_DIM)
    value_heads = value_rows.reshape(key_count, HEADS, HEAD_DIM)
    scores = jnp.einsum("qhd,khd->hqk", query_heads, key_heads, preferred_element_type=jnp.float32)
    scores = scores * (1.0 / math.sqrt(HEAD_DIM))
    scores = jnp.where(allowed[None], scores, NEG_LARGE)
    highest = jnp.max(scores, axis=-1, keepdims=True)
    exponent = jnp.exp(scores - highest)
    totals = jnp.sum(exponent, axis=-1, keepdims=True)
    weights = (exponent / totals).astype(jnp.bfloat16)
    mixture = jnp.einsum("hqk,khd->qhd", weights, value_heads, preferred_element_type=jnp.float32)
    return mixture.astype(jnp.bfloat16).reshape(query_count, HEADS * HEAD_DIM)


def plain(queries, key_value, keep, windows, gate, out_weight):
    frames_here = queries.shape[1]
    spots = queries.shape[2]
    features = queries.shape[3]
    model_width = gate.shape[1]
    slab_index = lax.axis_index("slab")
    stream_index = lax.axis_index("owner")
    request = stream_index // 2
    branch = stream_index % 2
    frames_total = frames_here * lax.axis_size("slab")
    window = lax.dynamic_index_in_dim(windows, request, 0, keepdims=False)
    gate_row = lax.dynamic_index_in_dim(gate, request, 0, keepdims=False)
    keep_flag = lax.dynamic_index_in_dim(keep, request, 0, keepdims=False)
    factor = jnp.where(branch == 1, keep_flag, 1)
    padded = padded_2(key_value, (("slab", 2),), HALO)
    allowed = window_mask(window, slab_index, frames_here, frames_total, spots)
    branch_rows = frames_here * spots
    query_rows = queries[0].reshape(branch_rows, features)
    key_rows = padded[0, 0].reshape(-1, features)
    value_rows = padded[1, 0].reshape(-1, features)
    operands = (query_rows, key_rows, value_rows)
    attended_rows = attend(operands[0], operands[1], operands[2], allowed)
    quad = ("groups", "slab")
    parts = lax.axis_size("groups") * lax.axis_size("slab")
    place = lax.axis_index("groups") * lax.axis_size("slab") + slab_index
    width = model_width // parts
    own_columns = lax.dynamic_slice_in_dim(out_weight, place * width, width, 1)
    weight_part = lax.all_gather(own_columns, "owner", axis=0, tiled=True)
    all_rows = lax.all_gather(attended_rows, quad, axis=0, tiled=True)
    scaled_gate = gate_row * factor.astype(jnp.float32)
    gates = lax.all_to_all(
        jnp.broadcast_to(scaled_gate.reshape(parts, 1, width), (parts, 8, width)),
        quad, split_axis=0, concat_axis=0, tiled=True,
    )
    product = jnp.dot(all_rows, weight_part, preferred_element_type=jnp.float32)
    product = product.reshape(parts, branch_rows, width) * gates[:, :1]
    scaled = product.astype(jnp.bfloat16).reshape(parts * branch_rows, width)
    result = lax.all_to_all(scaled, quad, split_axis=0, concat_axis=1, tiled=True)
    return result.reshape((1, frames_here, spots, model_width))


def fused_kernel(
    query_hbm, kv_hbm, weight_hbm, gate_hbm, keep_hbm, windows_hbm, out_ref,
    keep_ref, windows_ref,
    query, keys, values, weight, rows, finished, gates, gate_own, bias,
    load_sems, halo_send, halo_recv, gate_send, gate_recv, own_weight,
    z_recv, near_recv, far_recv, side_send, up_send, down_send, mate_send,
    rows_recv, pair_recv, rows_send, cols_recv, cols_send, own_out,
):
    group = lax.axis_index("groups")
    owner = lax.axis_index("owner")
    slab = lax.axis_index("slab")
    line, side = owner // 2, owner % 2
    lines = lax.axis_size("owner") // 2
    frames, spots, features = keys.shape[0] - HALO, keys.shape[1], keys.shape[2]
    tokens = frames * spots
    pieces, owners, depth, _ = weight.shape
    batches = rows.shape[0]
    span = features // batches
    quarter = pieces * PIECE
    place = group * 2 + slab
    across = (1 - group) * 2 + slab
    beside = group * 2 + 1 - slab
    corner = (1 - group) * 2 + 1 - slab
    to_side = {"owner": owner + 1 - 2 * side}
    to_up = {"owner": owner + 2}
    to_down = {"owner": owner - 2}
    to_across = {"groups": 1 - group}
    to_beside = {"slab": 1 - slab}
    to_corner = {"groups": 1 - group, "slab": 1 - slab}
    has_up = line + 1 < lines
    has_down = line > 0

    def remote(source, target, send, recv, device):
        return pltpu.make_async_remote_copy(
            src_ref=source, dst_ref=target, send_sem=send, recv_sem=recv,
            device_id=device, device_id_type=pl.DeviceIdType.MESH,
        )

    barrier = pltpu.get_barrier_semaphore()
    for device in (to_side, to_across, to_beside, to_corner):
        pl.semaphore_signal(barrier, inc=1, device_id=device, device_id_type=pl.DeviceIdType.MESH)

    @pl.when(has_up)
    def _():
        pl.semaphore_signal(barrier, inc=1, device_id=to_up, device_id_type=pl.DeviceIdType.MESH)

    @pl.when(has_down)
    def _():
        pl.semaphore_signal(barrier, inc=1, device_id=to_down, device_id_type=pl.DeviceIdType.MESH)

    loads = (
        pltpu.make_async_copy(query_hbm, query, load_sems.at[0]),
        pltpu.make_async_copy(kv_hbm.at[0], keys.at[pl.ds(0, frames)], load_sems.at[1]),
        pltpu.make_async_copy(kv_hbm.at[1], values.at[pl.ds(0, frames)], load_sems.at[2]),
        pltpu.make_async_copy(gate_hbm, gate_own, load_sems.at[3]),
    )
    settings = (
        pltpu.make_async_copy(keep_hbm, keep_ref, load_sems.at[4]),
        pltpu.make_async_copy(windows_hbm, windows_ref, load_sems.at[5]),
    )
    for load in settings + loads:
        load.start()
    pl.semaphore_wait(barrier, 4 + has_up.astype(jnp.int32) + has_down.astype(jnp.int32))

    def columns(index):
        return pl.ds(pl.multiple_of(place * quarter + index * PIECE, PIECE), PIECE)

    edge = (1 - slab) * (frames - 1)
    halos = (
        remote(kv_hbm.at[0, edge], keys.at[frames], halo_send.at[0], halo_recv.at[0], to_beside),
        remote(kv_hbm.at[1, edge], values.at[frames], halo_send.at[1], halo_recv.at[1], to_beside),
    )
    for halo in halos:
        halo.start()

    def own_copy(index, source):
        return remote(source, weight.at[index, owner], side_send, near_recv.at[index], to_side)

    def side_copy(index, at, source):
        return remote(source, weight.at[index, 2 * at + side], side_send, far_recv.at[index], to_side)

    def up_copy(index, at, source):
        return remote(source, weight.at[index, 2 * at + side], up_send, z_recv.at[index, at], to_up)

    def down_copy(index, at, source):
        return remote(source, weight.at[index, 2 * at + side], down_send, z_recv.at[index, at], to_down)

    for index in range(pieces):
        mine = weight_hbm.at[:, columns(index)]
        own_copy(index, mine).start()

        @pl.when(has_up)
        def _():
            up_copy(index, line, mine).start()

        @pl.when(has_down)
        def _():
            down_copy(index, line, mine).start()

        pltpu.make_async_copy(mine, weight.at[index, owner], own_weight).start()
    gate_copy = remote(gates.at[group], gates.at[group], gate_send, gate_recv, to_across)

    paired = lines % 2 == 0
    mate = line + 1 - 2 * (line % 2)
    to_mate = {"owner": owner + 2 - 4 * (line % 2)}

    def balanced(index):
        return 2 * index >= pieces if paired else index < 0

    def mate_copy(index):
        source = 2 * line + 1 - side
        block = weight.at[index, source]
        return remote(block, block, mate_send, far_recv.at[index], to_mate)

    def forward(index, apart):
        below, above = line - apart, line + apart

        @pl.when(below >= 0)
        def _():
            block = weight.at[index, 2 * below + side]
            up_copy(index, below, block).wait_recv()

            @pl.when(has_up)
            def _():
                up_copy(index, below, block).start()

            @pl.when(jnp.logical_not(balanced(index) & (below == mate)))
            def _():
                side_copy(index, below, block).start()

        @pl.when(above < lines)
        def _():
            block = weight.at[index, 2 * above + side]
            down_copy(index, above, block).wait_recv()

            @pl.when(has_down)
            def _():
                down_copy(index, above, block).start()

            @pl.when(jnp.logical_not(balanced(index) & (above == mate)))
            def _():
                side_copy(index, above, block).start()

    def within(index, count):
        return (index >= 0) & (index < count)

    def near_wait(index):
        block = weight.at[index, 2 * line + 1 - side]
        remote(block, block, side_send, near_recv.at[index], to_side).wait_recv()

    def mate_step(index):
        @pl.when(within(index, pieces) & balanced(index))
        def _():
            near_wait(index)
            mate_copy(index).start()

    def forward_steps(step, first=0, last=0):
        for apart in range(last or lines - 1, first, -1):
            index = step - LAG * apart

            @pl.when(within(index, pieces))
            def _():
                forward(index, apart)

    def places(ids):
        frame = sum((ids >= spots * step).astype(jnp.int32) for step in range(1, frames + HALO))
        spot = ids - frame * spots
        row = sum((spot >= WB * step).astype(jnp.int32) for step in range(1, spots // WB))
        return frame, row, spot - row * WB

    for load in settings:
        load.wait()
    request = owner // 2
    query_frame, query_row, query_column = places(lax.broadcasted_iota(jnp.int32, (tokens, 1), 0))
    key_at, key_row, key_column = places(lax.broadcasted_iota(jnp.int32, (1, tokens + spots), 1))
    halo_frame = frames - slab
    key_frame = jnp.where(key_at < frames, key_at + slab * frames, halo_frame)
    allowed = jnp.abs(query_frame + slab * frames - key_frame) <= windows_ref[request, 0]
    allowed = allowed & (jnp.abs(query_row - key_row) <= windows_ref[request, 1])
    allowed = allowed & (jnp.abs(query_column - key_column) <= windows_ref[request, 2])
    bias[...] = jnp.where(allowed, 0.0, NEG_LARGE)

    for load in loads:
        load.wait()
    factor = jnp.where(owner % 2 == 1, keep_ref[request], 1).astype(jnp.float32)
    gates[group] = jnp.broadcast_to(gate_own[pl.ds(request, 1), :] * factor, gates.shape[1:])
    for halo in halos:
        halo.wait_recv()

    def rows_copy(batch, origin, recv, device):
        block = rows.at[batch, origin]
        return remote(block, block, rows_send, recv, device)

    def attend_batch(batch, carry):
        for head in range(span // HEAD_DIM):
            lanes = pl.ds(pl.multiple_of(batch * span + head * HEAD_DIM, HEAD_DIM), HEAD_DIM)
            key_head = keys[:, :, lanes].reshape(-1, HEAD_DIM)
            value_head = values[:, :, lanes].reshape(-1, HEAD_DIM)
            scores = lax.dot_general(
                query[:, lanes], key_head, (((1,), (1,)), ((), ())),
                preferred_element_type=jnp.float32,
            )
            scores = scores * (1.0 / math.sqrt(HEAD_DIM)) + bias[...]
            exponent = jnp.exp(scores - jnp.max(scores, axis=-1, keepdims=True))
            totals = jnp.sum(exponent, axis=-1, keepdims=True)
            mixing = (exponent * (1.0 / totals)).astype(jnp.bfloat16)
            mixture = jnp.dot(mixing, value_head, preferred_element_type=jnp.float32)
            rows[batch, place, :, head * HEAD_DIM:(head + 1) * HEAD_DIM] = mixture.astype(jnp.bfloat16)
        rows_copy(batch, place, rows_recv.at[batch], to_across).start()
        rows_copy(batch, place, pair_recv.at[0], to_beside).start()

        mate_step(batch - MATE_LAG)
        relay_step(batch - RELAY_LAG)
        forward_steps(batch)
        return carry

    def relay_step(batch):
        @pl.when(within(batch, batches))
        def _():
            rows_copy(batch, across, rows_recv.at[batch], to_across).wait_recv()
            rows_copy(batch, across, pair_recv.at[1], to_beside).start()

    def forward_round(step, carry):
        mate_step(step - MATE_LAG)
        relay_step(step - RELAY_LAG)
        forward_steps(step)
        return carry

    lax.fori_loop(0, batches, attend_batch, 0)
    gate_copy.start()
    lax.fori_loop(batches, PROJECT_LAG, forward_round, 0)

    def cols_copy(index, slot, device):
        return remote(finished.at[index, slot], out_ref.at[:, columns(index)],
                      cols_send, cols_recv.at[place], device)

    def product(index, receiver, holder):
        whole = weight[index].reshape(owners * depth, PIECE)
        total = None
        for batch in range(batches):
            part = jnp.dot(rows[batch, receiver], whole[batch * span:(batch + 1) * span],
                           preferred_element_type=jnp.float32)
            total = part if total is None else total + part
        return (total * gates[holder, :, columns(index)][0:1]).astype(jnp.bfloat16)

    def receive_place(index):
        finished[index, 3] = product(index, place, group)
        pltpu.make_async_copy(finished.at[index, 3], out_ref.at[:, columns(index)], own_out).start()

    def serve(index, slot):
        receiver, holder, device = ((across, 1 - group, to_across), (corner, 1 - group, to_corner), (beside, group, to_beside))[slot]
        finished[index, slot] = product(index, receiver, holder)
        cols_copy(index, slot, device).start()

    def project(step, carry):
        index = step - PROJECT_LAG
        mate_step(step - MATE_LAG)
        relay_step(step - RELAY_LAG)

        @pl.when(index == 0)
        def _():
            gate_copy.wait_recv()
            for at, origin in enumerate((beside, corner)):
                every = rows.at[:, origin]
                remote(every, every, rows_send, pair_recv.at[at], to_beside).wait_recv()
            mine = weight.at[:, owner]
            pltpu.make_async_copy(mine, mine, own_weight).wait()

        @pl.when(jnp.logical_not(balanced(index)))
        def _():
            near_wait(index)

        if lines > 1:
            others = weight.at[index, pl.ds(0, lines - 1)]
            remote(others, others, side_send, far_recv.at[index], to_side).wait_recv()
        serve(index, 0)
        forward_steps(step, 1)
        serve(index, 1)
        forward_steps(step, 0, 1)
        serve(index, 2)

        @pl.when(index > 0)
        def _():
            receive_place(index - 1)

        return carry

    lax.fori_loop(PROJECT_LAG, PROJECT_LAG + pieces, project, 0)
    receive_place(pieces - 1)

    def sent(blocks, send):
        remote(blocks, blocks, send, near_recv.at[0], to_side).wait_send()

    if paired:
        sent(weight.at[pl.ds(0, pieces // 2), pl.ds(0, owners - 1)], side_send)
        sent(weight.at[pl.ds(0, pieces // 2), 0], mate_send)
    else:
        sent(weight.at[:, pl.ds(0, lines)], side_send)
    for at in range(lines):
        if at + 1 < lines:
            @pl.when(line == at)
            def _():
                sent(weight.at[:, pl.ds(0, at + 1)], up_send)
        if at > 0:
            @pl.when(line == at)
            def _():
                sent(weight.at[:, pl.ds(0, lines - at)], down_send)
    for halo in halos:
        halo.wait_send()
    gate_copy.wait_send()
    sent(rows.at[:, pl.ds(0, 3)], rows_send)
    sent(finished.at[:, pl.ds(0, 3)], cols_send)

    def quarter_of(origin):
        return out_ref.at[:, pl.ds(pl.multiple_of(origin * quarter, PIECE), quarter)]

    pltpu.make_async_copy(quarter_of(place), quarter_of(place), own_out).wait()
    for origin in (beside, across, corner):
        remote(quarter_of(origin), quarter_of(origin), cols_send, cols_recv.at[origin], to_across).wait_recv()


def fused(queries, key_value, keep, windows, gate, out_weight):
    frames, spots, features = queries.shape[1:]
    model_width = gate.shape[1]
    owners = lax.axis_size("owner")
    tokens = frames * spots
    depth = out_weight.shape[0]
    pieces = model_width // 4 // PIECE
    span = HEAD_GROUP * HEAD_DIM
    batches = features // span
    lines = owners // 2
    bf16 = jnp.bfloat16
    dma = pltpu.SemaphoreType.DMA
    whole = pl.BlockSpec(memory_space=pl.ANY)
    result = pl.pallas_call(
        fused_kernel,
        out_shape=pltpu.VMEM((tokens, model_width), bf16),
        in_specs=[whole] * 6,
        out_specs=whole,
        scratch_shapes=[
            pltpu.SMEM(keep.shape, jnp.int32),
            pltpu.SMEM(windows.shape, jnp.int32),
            pltpu.VMEM((tokens, features), bf16),
            pltpu.VMEM((frames + HALO, spots, features), bf16),
            pltpu.VMEM((frames + HALO, spots, features), bf16),
            pltpu.VMEM((pieces, owners, depth, PIECE), bf16),
            pltpu.VMEM((batches, 4, tokens, span), bf16),
            pltpu.VMEM((pieces, 4, tokens, PIECE), bf16),
            pltpu.VMEM((2, 8, model_width), jnp.float32),
            pltpu.VMEM(gate.shape, jnp.float32),
            pltpu.VMEM((tokens, tokens + spots), jnp.float32),
            dma((6,)), dma((2,)), dma((2,)), dma, dma, dma,
            dma((pieces, lines)), dma((pieces,)), dma((pieces,)), dma, dma, dma, dma,
            dma((batches,)), dma((2,)), dma,
            dma((4,)), dma, dma,
        ],
        compiler_params=pltpu.CompilerParams(
            collective_id=0, has_side_effects=True, vmem_limit_bytes=56 * 2**20,
        ),
    )(
        queries.reshape(tokens, features), key_value.reshape(2, frames, spots, features),
        out_weight, gate, keep, windows,
    )
    return result.reshape(1, frames, spots, model_width)


def on_device(queries, key_value, keep, windows, gate, out_weight):
    frames, spots, features = queries.shape[1:]
    fits = (
        lax.axis_size("slab") == 2
        and lax.axis_size("groups") == 2
        and lax.axis_size("owner") % 2 == 0
        and out_weight.shape[0] % 16 == 0
        and spots % 16 == 0
        and spots % WB == 0
        and features % (HEAD_GROUP * HEAD_DIM) == 0
        and gate.shape[1] % (8 * PIECE) == 0
    )
    chosen = fused if fits else plain
    return chosen(queries, key_value, keep, windows, gate, out_weight)


def solution(mesh):
    placed = (
        P(("groups", "owner"), "slab", None, None),
        P(None, ("groups", "owner"), "slab", None, None),
        P("groups"),
        P("groups", None),
        P("groups", None),
        P("owner", None),
    )
    return jax.shard_map(
        on_device,
        mesh=mesh,
        in_specs=placed,
        out_specs=P(("groups", "owner"), "slab", None, None),
        check_vma=False,
    )
```

```python
import math

import jax
import jax.numpy as jnp
from jax import lax
from jax.experimental import pallas as pl
from jax.experimental.pallas import tpu as pltpu
from jax.sharding import PartitionSpec as P

HEADS = 20
HEAD_DIM = 128
WB = 14
HALO = 1


NEG_LARGE = -1e30
PIECE = 128
HEAD_GROUP = 4
LAG = 2
MATE_LAG = 6
RELAY_LAG = 4
PROJECT_LAG = 8


def padded_2(cells, sides, width):
    for axis, dim in sides:
        count = lax.axis_size(axis)
        ends = count - 1
        head = lax.slice_in_dim(cells, 0, width, axis=dim)
        tail = lax.slice_in_dim(cells, cells.shape[dim] - width, cells.shape[dim], axis=dim)
        cells = jnp.concatenate(
            [
                lax.ppermute(tail, axis, [(i, (i + 1) % count) for i in range(ends)]),
                cells,
                lax.ppermute(head, axis, [((i + 1) % count, i) for i in range(ends)]),
            ],
            axis=dim,
        )
    return cells


def window_mask(window, slab_index, frames_here, frames_total, spots):
    query_ids = jnp.arange(frames_here * spots, dtype=jnp.int32)
    key_ids = jnp.arange((frames_here + 2 * HALO) * spots, dtype=jnp.int32)
    query_frame = slab_index * frames_here + query_ids // spots
    key_frame = slab_index * frames_here - HALO + key_ids // spots
    query_row = query_ids % spots // WB
    key_row = key_ids % spots // WB
    query_column = query_ids % spots % WB
    key_column = key_ids % spots % WB
    inside = (key_frame >= 0) & (key_frame < frames_total)
    allowed = jnp.abs(query_frame[:, None] - key_frame[None, :]) <= window[0]
    allowed = allowed & (jnp.abs(query_row[:, None] - key_row[None, :]) <= window[1])
    allowed = allowed & (jnp.abs(query_column[:, None] - key_column[None, :]) <= window[2])
    return allowed & inside[None, :]


def attend(query_rows, key_rows, value_rows, allowed):
    query_count = query_rows.shape[0]
    key_count = key_rows.shape[0]
    query_heads = query_rows.reshape(query_count, HEADS, HEAD_DIM)
    key_heads = key_rows.reshape(key_count, HEADS, HEAD_DIM)
    value_heads = value_rows.reshape(key_count, HEADS, HEAD_DIM)
    scores = jnp.einsum("qhd,khd->hqk", query_heads, key_heads, preferred_element_type=jnp.float32)
    scores = scores * (1.0 / math.sqrt(HEAD_DIM))
    scores = jnp.where(allowed[None], scores, NEG_LARGE)
    highest = jnp.max(scores, axis=-1, keepdims=True)
    exponent = jnp.exp(scores - highest)
    totals = jnp.sum(exponent, axis=-1, keepdims=True)
    weights = (exponent / totals).astype(jnp.bfloat16)
    mixture = jnp.einsum("hqk,khd->qhd", weights, value_heads, preferred_element_type=jnp.float32)
    return mixture.astype(jnp.bfloat16).reshape(query_count, HEADS * HEAD_DIM)


def plain(queries, key_value, keep, windows, gate, out_weight):
    frames_here = queries.shape[1]
    spots = queries.shape[2]
    features = queries.shape[3]
    model_width = gate.shape[1]
    slab_index = lax.axis_index("slab")
    stream_index = lax.axis_index("owner")
    request = stream_index // 2
    branch = stream_index % 2
    frames_total = frames_here * lax.axis_size("slab")
    window = lax.dynamic_index_in_dim(windows, request, 0, keepdims=False)
    gate_row = lax.dynamic_index_in_dim(gate, request, 0, keepdims=False)
    keep_flag = lax.dynamic_index_in_dim(keep, request, 0, keepdims=False)
    factor = jnp.where(branch == 1, keep_flag, 1)
    padded = padded_2(key_value, (("slab", 2),), HALO)
    allowed = window_mask(window, slab_index, frames_here, frames_total, spots)
    branch_rows = frames_here * spots
    query_rows = queries[0].reshape(branch_rows, features)
    key_rows = padded[0, 0].reshape(-1, features)
    value_rows = padded[1, 0].reshape(-1, features)
    operands = (query_rows, key_rows, value_rows)
    attended_rows = attend(operands[0], operands[1], operands[2], allowed)
    quad = ("groups", "slab")
    parts = lax.axis_size("groups") * lax.axis_size("slab")
    place = lax.axis_index("groups") * lax.axis_size("slab") + slab_index
    width = model_width // parts
    own_columns = lax.dynamic_slice_in_dim(out_weight, place * width, width, 1)
    weight_part = lax.all_gather(own_columns, "owner", axis=0, tiled=True)
    all_rows = lax.all_gather(attended_rows, quad, axis=0, tiled=True)
    scaled_gate = gate_row * factor.astype(jnp.float32)
    gates = lax.all_to_all(
        jnp.broadcast_to(scaled_gate.reshape(parts, 1, width), (parts, 8, width)),
        quad, split_axis=0, concat_axis=0, tiled=True,
    )
    product = jnp.dot(all_rows, weight_part, preferred_element_type=jnp.float32)
    product = product.reshape(parts, branch_rows, width) * gates[:, :1]
    scaled = product.astype(jnp.bfloat16).reshape(parts * branch_rows, width)
    result = lax.all_to_all(scaled, quad, split_axis=0, concat_axis=1, tiled=True)
    return result.reshape((1, frames_here, spots, model_width))


def fused_kernel(
    query_hbm, kv_hbm, weight_hbm, gate_hbm, keep_hbm, windows_hbm, out_ref,
    keep_ref, windows_ref,
    query, keys, values, weight, rows, finished, gates, gate_own, bias,
    load_sems, halo_send, halo_recv, gate_send, gate_recv, own_weight,
    z_recv, near_recv, far_recv, side_send, up_send, down_send, mate_send,
    rows_recv, pair_recv, rows_send, cols_recv, cols_send, own_out,
):
    group = lax.axis_index("groups")
    owner = lax.axis_index("owner")
    slab = lax.axis_index("slab")
    line, side = owner // 2, owner % 2
    lines = lax.axis_size("owner") // 2
    frames, spots, features = keys.shape[0] - HALO, keys.shape[1], keys.shape[2]
    tokens = frames * spots
    pieces, owners, depth, _ = weight.shape
    batches = rows.shape[0]
    span = features // batches
    quarter = pieces * PIECE
    place = group * 2 + slab
    across = (1 - group) * 2 + slab
    beside = group * 2 + 1 - slab
    corner = (1 - group) * 2 + 1 - slab
    to_side = {"owner": owner + 1 - 2 * side}
    to_up = {"owner": owner + 2}
    to_down = {"owner": owner - 2}
    to_across = {"groups": 1 - group}
    to_beside = {"slab": 1 - slab}
    to_corner = {"groups": 1 - group, "slab": 1 - slab}
    has_up = line + 1 < lines
    has_down = line > 0

    def remote(source, target, send, recv, device):
        return pltpu.make_async_remote_copy(
            src_ref=source, dst_ref=target, send_sem=send, recv_sem=recv,
            device_id=device, device_id_type=pl.DeviceIdType.MESH,
        )

    barrier = pltpu.get_barrier_semaphore()
    for device in (to_side, to_across, to_beside, to_corner):
        pl.semaphore_signal(barrier, inc=1, device_id=device, device_id_type=pl.DeviceIdType.MESH)

    @pl.when(has_up)
    def _():
        pl.semaphore_signal(barrier, inc=1, device_id=to_up, device_id_type=pl.DeviceIdType.MESH)

    @pl.when(has_down)
    def _():
        pl.semaphore_signal(barrier, inc=1, device_id=to_down, device_id_type=pl.DeviceIdType.MESH)

    loads = (
        pltpu.make_async_copy(query_hbm, query, load_sems.at[0]),
        pltpu.make_async_copy(kv_hbm.at[0], keys.at[pl.ds(0, frames)], load_sems.at[1]),
        pltpu.make_async_copy(kv_hbm.at[1], values.at[pl.ds(0, frames)], load_sems.at[2]),
        pltpu.make_async_copy(gate_hbm, gate_own, load_sems.at[3]),
    )
    settings = (
        pltpu.make_async_copy(keep_hbm, keep_ref, load_sems.at[4]),
        pltpu.make_async_copy(windows_hbm, windows_ref, load_sems.at[5]),
    )
    pl.semaphore_wait(barrier, 4 + has_up.astype(jnp.int32) + has_down.astype(jnp.int32))

    def columns(index):
        return pl.ds(pl.multiple_of(place * quarter + index * PIECE, PIECE), PIECE)

    edge = (1 - slab) * (frames - 1)
    halos = (
        remote(kv_hbm.at[0, edge], keys.at[frames], halo_send.at[0], halo_recv.at[0], to_beside),
        remote(kv_hbm.at[1, edge], values.at[frames], halo_send.at[1], halo_recv.at[1], to_beside),
    )
    for halo in halos:
        halo.start()

    def own_copy(index, source):
        return remote(source, weight.at[index, owner], side_send, near_recv.at[index], to_side)

    def side_copy(index, at, source):
        return remote(source, weight.at[index, 2 * at + side], side_send, far_recv.at[index], to_side)

    def up_copy(index, at, source):
        return remote(source, weight.at[index, 2 * at + side], up_send, z_recv.at[index, at], to_up)

    def down_copy(index, at, source):
        return remote(source, weight.at[index, 2 * at + side], down_send, z_recv.at[index, at - 1], to_down)

    for index in range(pieces):
        mine = weight_hbm.at[:, columns(index)]
        own_copy(index, mine).start()

        @pl.when(has_up)
        def _():
            up_copy(index, line, mine).start()

        @pl.when(has_down)
        def _():
            down_copy(index, line, mine).start()

    for load in settings + loads:
        load.start()
    for index in range(pieces):
        pltpu.make_async_copy(weight_hbm.at[:, columns(index)], weight.at[index, owner], own_weight).start()
    gate_copy = remote(gates.at[group], gates.at[group], gate_send, gate_recv, to_across)

    paired = lines % 2 == 0
    mate = line + 1 - 2 * (line % 2)
    to_mate = {"owner": owner + 2 - 4 * (line % 2)}

    def balanced(index):
        return 2 * index >= pieces if paired else index < 0

    def mate_copy(index):
        source = 2 * line + 1 - side
        block = weight.at[index, source]
        return remote(block, block, mate_send, far_recv.at[index], to_mate)

    def forward(index, apart):
        below, above = line - apart, line + apart

        @pl.when(below >= 0)
        def _():
            block = weight.at[index, 2 * below + side]
            up_copy(index, below, block).wait_recv()

            @pl.when(has_up)
            def _():
                up_copy(index, below, block).start()

            @pl.when(jnp.logical_not(balanced(index) & (below == mate)))
            def _():
                side_copy(index, below, block).start()

        @pl.when(above < lines)
        def _():
            block = weight.at[index, 2 * above + side]
            down_copy(index, above, block).wait_recv()

            @pl.when(has_down)
            def _():
                down_copy(index, above, block).start()

            @pl.when(jnp.logical_not(balanced(index) & (above == mate)))
            def _():
                side_copy(index, above, block).start()

    def within(index, count):
        return (index >= 0) & (index < count)

    def near_wait(index):
        block = weight.at[index, 2 * line + 1 - side]
        remote(block, block, side_send, near_recv.at[index], to_side).wait_recv()

    def mate_step(index):
        @pl.when(within(index, pieces) & balanced(index))
        def _():
            near_wait(index)
            mate_copy(index).start()

    def forward_steps(step, first=0, last=0):
        for apart in range(last or lines - 1, first, -1):
            index = step - LAG * apart

            @pl.when(within(index, pieces))
            def _():
                forward(index, apart)

    def places(ids):
        frame = sum((ids >= spots * step).astype(jnp.int32) for step in range(1, frames + HALO))
        spot = ids - frame * spots
        row = sum((spot >= WB * step).astype(jnp.int32) for step in range(1, spots // WB))
        return frame, row, spot - row * WB

    for load in settings:
        load.wait()
    request = owner // 2
    query_frame, query_row, query_column = places(lax.broadcasted_iota(jnp.int32, (tokens, 1), 0))
    key_at, key_row, key_column = places(lax.broadcasted_iota(jnp.int32, (1, tokens + spots), 1))
    halo_frame = frames - slab
    key_frame = jnp.where(key_at < frames, key_at + slab * frames, halo_frame)
    allowed = jnp.abs(query_frame + slab * frames - key_frame) <= windows_ref[request, 0]
    allowed = allowed & (jnp.abs(query_row - key_row) <= windows_ref[request, 1])
    allowed = allowed & (jnp.abs(query_column - key_column) <= windows_ref[request, 2])
    bias[...] = jnp.where(allowed, 0.0, NEG_LARGE)

    for load in loads:
        load.wait()
    factor = jnp.where(owner % 2 == 1, keep_ref[request], 1).astype(jnp.float32)
    gates[group] = jnp.broadcast_to(gate_own[pl.ds(request, 1), :] * factor, gates.shape[1:])
    for halo in halos:
        halo.wait_recv()

    def rows_copy(batch, origin, recv, device):
        block = rows.at[batch, origin]
        return remote(block, block, rows_send, recv, device)

    def attend_batch(batch, carry):
        for head in range(span // HEAD_DIM):
            lanes = pl.ds(pl.multiple_of(batch * span + head * HEAD_DIM, HEAD_DIM), HEAD_DIM)
            key_head = keys[:, :, lanes].reshape(-1, HEAD_DIM)
            value_head = values[:, :, lanes].reshape(-1, HEAD_DIM)
            scores = lax.dot_general(
                query[:, lanes], key_head, (((1,), (1,)), ((), ())),
                preferred_element_type=jnp.float32,
            )
            scores = scores * (1.0 / math.sqrt(HEAD_DIM)) + bias[...]
            exponent = jnp.exp(scores - jnp.max(scores, axis=-1, keepdims=True))
            totals = jnp.sum(exponent, axis=-1, keepdims=True)
            mixing = (exponent * (1.0 / totals)).astype(jnp.bfloat16)
            mixture = jnp.dot(mixing, value_head, preferred_element_type=jnp.float32)
            rows[batch, place, :, head * HEAD_DIM:(head + 1) * HEAD_DIM] = mixture.astype(jnp.bfloat16)
        rows_copy(batch, place, rows_recv.at[batch], to_across).start()
        rows_copy(batch, place, pair_recv.at[0], to_beside).start()

        mate_step(batch - MATE_LAG)
        relay_step(batch - RELAY_LAG)
        forward_steps(batch)
        return carry

    def relay_step(batch):
        @pl.when(within(batch, batches))
        def _():
            rows_copy(batch, across, rows_recv.at[batch], to_across).wait_recv()
            rows_copy(batch, across, pair_recv.at[1], to_beside).start()

    def forward_round(step, carry):
        mate_step(step - MATE_LAG)
        relay_step(step - RELAY_LAG)
        forward_steps(step)
        return carry

    lax.fori_loop(0, batches, attend_batch, 0)
    gate_copy.start()
    lax.fori_loop(batches, PROJECT_LAG, forward_round, 0)

    def cols_copy(index, slot, device):
        return remote(finished.at[index, slot], out_ref.at[:, columns(index)],
                      cols_send, cols_recv.at[place], device)

    def product(index, receiver, holder):
        whole = weight[index].reshape(owners * depth, PIECE)
        total = None
        for batch in range(batches):
            part = jnp.dot(rows[batch, receiver], whole[batch * span:(batch + 1) * span],
                           preferred_element_type=jnp.float32)
            total = part if total is None else total + part
        return (total * gates[holder, :, columns(index)][0:1]).astype(jnp.bfloat16)

    def receive_place(index):
        finished[index, 3] = product(index, place, group)
        pltpu.make_async_copy(finished.at[index, 3], out_ref.at[:, columns(index)], own_out).start()

    def serve(index, slot):
        receiver, holder, device = ((across, 1 - group, to_across), (corner, 1 - group, to_corner), (beside, group, to_beside))[slot]
        finished[index, slot] = product(index, receiver, holder)
        cols_copy(index, slot, device).start()

    def project(step, carry):
        index = step - PROJECT_LAG
        mate_step(step - MATE_LAG)
        relay_step(step - RELAY_LAG)

        @pl.when(index == 0)
        def _():
            gate_copy.wait_recv()
            for at, origin in enumerate((beside, corner)):
                every = rows.at[:, origin]
                remote(every, every, rows_send, pair_recv.at[at], to_beside).wait_recv()
            mine = weight.at[:, owner]
            pltpu.make_async_copy(mine, mine, own_weight).wait()

        @pl.when(jnp.logical_not(balanced(index)))
        def _():
            near_wait(index)

        if lines > 1:
            others = weight.at[index, pl.ds(0, lines - 1)]
            remote(others, others, side_send, far_recv.at[index], to_side).wait_recv()
        serve(index, 0)
        forward_steps(step, 1)
        serve(index, 1)
        forward_steps(step, 0, 1)
        serve(index, 2)

        @pl.when(index > 0)
        def _():
            receive_place(index - 1)

        return carry

    lax.fori_loop(PROJECT_LAG, PROJECT_LAG + pieces, project, 0)
    receive_place(pieces - 1)

    def sent(blocks, send):
        remote(blocks, blocks, send, near_recv.at[0], to_side).wait_send()

    if paired:
        sent(weight.at[pl.ds(0, pieces // 2), pl.ds(0, owners - 1)], side_send)
        sent(weight.at[pl.ds(0, pieces // 2), 0], mate_send)
    else:
        sent(weight.at[:, pl.ds(0, lines)], side_send)
    for at in range(lines):
        if at + 1 < lines:
            @pl.when(line == at)
            def _():
                sent(weight.at[:, pl.ds(0, at + 1)], up_send)
        if at > 0:
            @pl.when(line == at)
            def _():
                sent(weight.at[:, pl.ds(0, lines - at)], down_send)
    for halo in halos:
        halo.wait_send()
    gate_copy.wait_send()
    sent(rows.at[:, pl.ds(0, 3)], rows_send)
    sent(finished.at[:, pl.ds(0, 3)], cols_send)

    def quarter_of(origin):
        return out_ref.at[:, pl.ds(pl.multiple_of(origin * quarter, PIECE), quarter)]

    pltpu.make_async_copy(quarter_of(place), quarter_of(place), own_out).wait()
    for origin in (beside, across, corner):
        remote(quarter_of(origin), quarter_of(origin), cols_send, cols_recv.at[origin], to_across).wait_recv()


def fused(queries, key_value, keep, windows, gate, out_weight):
    frames, spots, features = queries.shape[1:]
    model_width = gate.shape[1]
    owners = lax.axis_size("owner")
    tokens = frames * spots
    depth = out_weight.shape[0]
    pieces = model_width // 4 // PIECE
    span = HEAD_GROUP * HEAD_DIM
    batches = features // span
    lines = owners // 2
    bf16 = jnp.bfloat16
    dma = pltpu.SemaphoreType.DMA
    whole = pl.BlockSpec(memory_space=pl.ANY)
    result = pl.pallas_call(
        fused_kernel,
        out_shape=pltpu.VMEM((tokens, model_width), bf16),
        in_specs=[whole] * 6,
        out_specs=whole,
        scratch_shapes=[
            pltpu.SMEM(keep.shape, jnp.int32),
            pltpu.SMEM(windows.shape, jnp.int32),
            pltpu.VMEM((tokens, features), bf16),
            pltpu.VMEM((frames + HALO, spots, features), bf16),
            pltpu.VMEM((frames + HALO, spots, features), bf16),
            pltpu.VMEM((pieces, owners, depth, PIECE), bf16),
            pltpu.VMEM((batches, 4, tokens, span), bf16),
            pltpu.VMEM((pieces, 4, tokens, PIECE), bf16),
            pltpu.VMEM((2, 8, model_width), jnp.float32),
            pltpu.VMEM(gate.shape, jnp.float32),
            pltpu.VMEM((tokens, tokens + spots), jnp.float32),
            dma((6,)), dma((2,)), dma((2,)), dma, dma, dma,
            dma((pieces, max(lines - 1, 1))), dma((pieces,)), dma((pieces,)), dma, dma, dma, dma,
            dma((batches,)), dma((2,)), dma,
            dma((4,)), dma, dma,
        ],
        compiler_params=pltpu.CompilerParams(
            collective_id=0, has_side_effects=True, vmem_limit_bytes=56 * 2**20,
        ),
    )(
        queries.reshape(tokens, features), key_value.reshape(2, frames, spots, features),
        out_weight, gate, keep, windows,
    )
    return result.reshape(1, frames, spots, model_width)


def on_device(queries, key_value, keep, windows, gate, out_weight):
    frames, spots, features = queries.shape[1:]
    fits = (
        lax.axis_size("slab") == 2
        and lax.axis_size("groups") == 2
        and lax.axis_size("owner") % 2 == 0
        and out_weight.shape[0] % 16 == 0
        and spots % 16 == 0
        and spots % WB == 0
        and features % (HEAD_GROUP * HEAD_DIM) == 0
        and gate.shape[1] % (8 * PIECE) == 0
    )
    chosen = fused if fits else plain
    return chosen(queries, key_value, keep, windows, gate, out_weight)


def solution(mesh):
    placed = (
        P(("groups", "owner"), "slab", None, None),
        P(None, ("groups", "owner"), "slab", None, None),
        P("groups"),
        P("groups", None),
        P("groups", None),
        P("owner", None),
    )
    return jax.shard_map(
        on_device,
        mesh=mesh,
        in_specs=placed,
        out_specs=P(("groups", "owner"), "slab", None, None),
        check_vma=False,
    )
```

```python
import math

import jax
import jax.numpy as jnp
from jax import lax
from jax.experimental import pallas as pl
from jax.experimental.pallas import tpu as pltpu
from jax.sharding import PartitionSpec as P

HEADS = 20
HEAD_DIM = 128
WB = 14
HALO = 1


NEG_LARGE = -1e30
PIECE = 128
HEAD_GROUP = 4
LAG = 2
MATE_LAG = 6
RELAY_LAG = 4
PROJECT_LAG = 8


def padded_2(cells, sides, width):
    for axis, dim in sides:
        count = lax.axis_size(axis)
        ends = count - 1
        head = lax.slice_in_dim(cells, 0, width, axis=dim)
        tail = lax.slice_in_dim(cells, cells.shape[dim] - width, cells.shape[dim], axis=dim)
        cells = jnp.concatenate(
            [
                lax.ppermute(tail, axis, [(i, (i + 1) % count) for i in range(ends)]),
                cells,
                lax.ppermute(head, axis, [((i + 1) % count, i) for i in range(ends)]),
            ],
            axis=dim,
        )
    return cells


def window_mask(window, slab_index, frames_here, frames_total, spots):
    query_ids = jnp.arange(frames_here * spots, dtype=jnp.int32)
    key_ids = jnp.arange((frames_here + 2 * HALO) * spots, dtype=jnp.int32)
    query_frame = slab_index * frames_here + query_ids // spots
    key_frame = slab_index * frames_here - HALO + key_ids // spots
    query_row = query_ids % spots // WB
    key_row = key_ids % spots // WB
    query_column = query_ids % spots % WB
    key_column = key_ids % spots % WB
    inside = (key_frame >= 0) & (key_frame < frames_total)
    allowed = jnp.abs(query_frame[:, None] - key_frame[None, :]) <= window[0]
    allowed = allowed & (jnp.abs(query_row[:, None] - key_row[None, :]) <= window[1])
    allowed = allowed & (jnp.abs(query_column[:, None] - key_column[None, :]) <= window[2])
    return allowed & inside[None, :]


def attend(query_rows, key_rows, value_rows, allowed):
    query_count = query_rows.shape[0]
    key_count = key_rows.shape[0]
    query_heads = query_rows.reshape(query_count, HEADS, HEAD_DIM)
    key_heads = key_rows.reshape(key_count, HEADS, HEAD_DIM)
    value_heads = value_rows.reshape(key_count, HEADS, HEAD_DIM)
    scores = jnp.einsum("qhd,khd->hqk", query_heads, key_heads, preferred_element_type=jnp.float32)
    scores = scores * (1.0 / math.sqrt(HEAD_DIM))
    scores = jnp.where(allowed[None], scores, NEG_LARGE)
    highest = jnp.max(scores, axis=-1, keepdims=True)
    exponent = jnp.exp(scores - highest)
    totals = jnp.sum(exponent, axis=-1, keepdims=True)
    weights = (exponent / totals).astype(jnp.bfloat16)
    mixture = jnp.einsum("hqk,khd->qhd", weights, value_heads, preferred_element_type=jnp.float32)
    return mixture.astype(jnp.bfloat16).reshape(query_count, HEADS * HEAD_DIM)


def plain(queries, key_value, keep, windows, gate, out_weight):
    frames_here = queries.shape[1]
    spots = queries.shape[2]
    features = queries.shape[3]
    model_width = gate.shape[1]
    slab_index = lax.axis_index("slab")
    stream_index = lax.axis_index("owner")
    request = stream_index // 2
    branch = stream_index % 2
    frames_total = frames_here * lax.axis_size("slab")
    window = lax.dynamic_index_in_dim(windows, request, 0, keepdims=False)
    gate_row = lax.dynamic_index_in_dim(gate, request, 0, keepdims=False)
    keep_flag = lax.dynamic_index_in_dim(keep, request, 0, keepdims=False)
    factor = jnp.where(branch == 1, keep_flag, 1)
    padded = padded_2(key_value, (("slab", 2),), HALO)
    allowed = window_mask(window, slab_index, frames_here, frames_total, spots)
    branch_rows = frames_here * spots
    query_rows = queries[0].reshape(branch_rows, features)
    key_rows = padded[0, 0].reshape(-1, features)
    value_rows = padded[1, 0].reshape(-1, features)
    operands = (query_rows, key_rows, value_rows)
    attended_rows = attend(operands[0], operands[1], operands[2], allowed)
    quad = ("groups", "slab")
    parts = lax.axis_size("groups") * lax.axis_size("slab")
    place = lax.axis_index("groups") * lax.axis_size("slab") + slab_index
    width = model_width // parts
    own_columns = lax.dynamic_slice_in_dim(out_weight, place * width, width, 1)
    weight_part = lax.all_gather(own_columns, "owner", axis=0, tiled=True)
    all_rows = lax.all_gather(attended_rows, quad, axis=0, tiled=True)
    scaled_gate = gate_row * factor.astype(jnp.float32)
    gates = lax.all_to_all(
        jnp.broadcast_to(scaled_gate.reshape(parts, 1, width), (parts, 8, width)),
        quad, split_axis=0, concat_axis=0, tiled=True,
    )
    product = jnp.dot(all_rows, weight_part, preferred_element_type=jnp.float32)
    product = product.reshape(parts, branch_rows, width) * gates[:, :1]
    scaled = product.astype(jnp.bfloat16).reshape(parts * branch_rows, width)
    result = lax.all_to_all(scaled, quad, split_axis=0, concat_axis=1, tiled=True)
    return result.reshape((1, frames_here, spots, model_width))


def fused_kernel(
    query_hbm, kv_hbm, weight_hbm, gate_hbm, keep_hbm, windows_hbm, out_ref,
    keep_ref, windows_ref,
    query, keys, values, weight, rows, finished, gates, gate_own, bias,
    load_sems, halo_send, halo_recv, gate_send, gate_recv, own_weight,
    z_recv, near_recv, far_recv, side_send, up_send, down_send, mate_send,
    rows_recv, pair_recv, rows_send, cols_recv, cols_send,
):
    group = lax.axis_index("groups")
    owner = lax.axis_index("owner")
    slab = lax.axis_index("slab")
    line, side = owner // 2, owner % 2
    lines = lax.axis_size("owner") // 2
    frames, spots, features = keys.shape[0] - HALO, keys.shape[1], keys.shape[2]
    tokens = frames * spots
    pieces, owners, depth, _ = weight.shape
    batches = rows.shape[0]
    span = features // batches
    quarter = pieces * PIECE
    place = group * 2 + slab
    across = (1 - group) * 2 + slab
    beside = group * 2 + 1 - slab
    corner = (1 - group) * 2 + 1 - slab
    to_side = {"owner": owner + 1 - 2 * side}
    to_up = {"owner": owner + 2}
    to_down = {"owner": owner - 2}
    to_across = {"groups": 1 - group}
    to_beside = {"slab": 1 - slab}
    to_corner = {"groups": 1 - group, "slab": 1 - slab}
    has_up = line + 1 < lines
    has_down = line > 0

    def remote(source, target, send, recv, device):
        return pltpu.make_async_remote_copy(
            src_ref=source, dst_ref=target, send_sem=send, recv_sem=recv,
            device_id=device, device_id_type=pl.DeviceIdType.MESH,
        )

    barrier = pltpu.get_barrier_semaphore()
    for device in (to_side, to_across, to_beside, to_corner):
        pl.semaphore_signal(barrier, inc=1, device_id=device, device_id_type=pl.DeviceIdType.MESH)

    @pl.when(has_up)
    def _():
        pl.semaphore_signal(barrier, inc=1, device_id=to_up, device_id_type=pl.DeviceIdType.MESH)

    @pl.when(has_down)
    def _():
        pl.semaphore_signal(barrier, inc=1, device_id=to_down, device_id_type=pl.DeviceIdType.MESH)

    loads = (
        pltpu.make_async_copy(query_hbm, query, load_sems.at[0]),
        pltpu.make_async_copy(kv_hbm.at[0], keys.at[pl.ds(0, frames)], load_sems.at[1]),
        pltpu.make_async_copy(kv_hbm.at[1], values.at[pl.ds(0, frames)], load_sems.at[2]),
        pltpu.make_async_copy(gate_hbm, gate_own, load_sems.at[3]),
    )
    settings = (
        pltpu.make_async_copy(keep_hbm, keep_ref, load_sems.at[4]),
        pltpu.make_async_copy(windows_hbm, windows_ref, load_sems.at[5]),
    )
    pl.semaphore_wait(barrier, 4 + has_up.astype(jnp.int32) + has_down.astype(jnp.int32))

    def columns(index):
        return pl.ds(pl.multiple_of(place * quarter + index * PIECE, PIECE), PIECE)

    edge = (1 - slab) * (frames - 1)
    halos = (
        remote(kv_hbm.at[0, edge], keys.at[frames], halo_send.at[0], halo_recv.at[0], to_beside),
        remote(kv_hbm.at[1, edge], values.at[frames], halo_send.at[1], halo_recv.at[1], to_beside),
    )
    for halo in halos:
        halo.start()

    def own_copy(index, source):
        return remote(source, weight.at[index, owner], side_send, near_recv.at[index], to_side)

    def side_copy(index, at, source):
        return remote(source, weight.at[index, 2 * at + side], side_send, far_recv.at[index], to_side)

    def up_copy(index, at, source):
        return remote(source, weight.at[index, 2 * at + side], up_send, z_recv.at[index, at], to_up)

    def down_copy(index, at, source):
        return remote(source, weight.at[index, 2 * at + side], down_send, z_recv.at[index, at - 1], to_down)

    for index in range(pieces):
        mine = weight_hbm.at[:, columns(index)]
        own_copy(index, mine).start()

        @pl.when(has_up)
        def _():
            up_copy(index, line, mine).start()

        @pl.when(has_down)
        def _():
            down_copy(index, line, mine).start()

    for load in settings + loads:
        load.start()
    for index in range(pieces):
        pltpu.make_async_copy(weight_hbm.at[:, columns(index)], weight.at[index, owner], own_weight).start()
    gate_copy = remote(gates.at[group], gates.at[group], gate_send, gate_recv, to_across)

    paired = lines % 2 == 0
    mate = line + 1 - 2 * (line % 2)
    to_mate = {"owner": owner + 2 - 4 * (line % 2)}

    def balanced(index):
        return 2 * index >= pieces if paired else index < 0

    def mate_copy(index):
        source = 2 * line + 1 - side
        block = weight.at[index, source]
        return remote(block, block, mate_send, far_recv.at[index], to_mate)

    def forward(index, apart):
        below, above = line - apart, line + apart

        @pl.when(below >= 0)
        def _():
            block = weight.at[index, 2 * below + side]
            up_copy(index, below, block).wait_recv()

            @pl.when(has_up)
            def _():
                up_copy(index, below, block).start()

            @pl.when(jnp.logical_not(balanced(index) & (below == mate)))
            def _():
                side_copy(index, below, block).start()

        @pl.when(above < lines)
        def _():
            block = weight.at[index, 2 * above + side]
            down_copy(index, above, block).wait_recv()

            @pl.when(has_down)
            def _():
                down_copy(index, above, block).start()

            @pl.when(jnp.logical_not(balanced(index) & (above == mate)))
            def _():
                side_copy(index, above, block).start()

    def within(index, count):
        return (index >= 0) & (index < count)

    def near_wait(index):
        block = weight.at[index, 2 * line + 1 - side]
        remote(block, block, side_send, near_recv.at[index], to_side).wait_recv()

    def mate_step(index):
        @pl.when(within(index, pieces) & balanced(index))
        def _():
            near_wait(index)
            mate_copy(index).start()

    def forward_steps(step, first=0, last=0):
        for apart in range(last or lines - 1, first, -1):
            index = step - LAG * apart

            @pl.when(within(index, pieces))
            def _():
                forward(index, apart)

    def places(ids):
        frame = sum((ids >= spots * step).astype(jnp.int32) for step in range(1, frames + HALO))
        spot = ids - frame * spots
        row = sum((spot >= WB * step).astype(jnp.int32) for step in range(1, spots // WB))
        return frame, row, spot - row * WB

    for load in settings:
        load.wait()
    request = owner // 2
    query_frame, query_row, query_column = places(lax.broadcasted_iota(jnp.int32, (tokens, 1), 0))
    key_at, key_row, key_column = places(lax.broadcasted_iota(jnp.int32, (1, tokens + spots), 1))
    halo_frame = frames - slab
    key_frame = jnp.where(key_at < frames, key_at + slab * frames, halo_frame)
    allowed = jnp.abs(query_frame + slab * frames - key_frame) <= windows_ref[request, 0]
    allowed = allowed & (jnp.abs(query_row - key_row) <= windows_ref[request, 1])
    allowed = allowed & (jnp.abs(query_column - key_column) <= windows_ref[request, 2])
    bias[...] = jnp.where(allowed, 0.0, NEG_LARGE)

    for load in loads:
        load.wait()
    factor = jnp.where(owner % 2 == 1, keep_ref[request], 1).astype(jnp.float32)
    gates[group] = jnp.broadcast_to(gate_own[pl.ds(request, 1), :] * factor, gates.shape[1:])
    for halo in halos:
        halo.wait_recv()

    def rows_copy(batch, origin, recv, device):
        block = rows.at[batch, origin]
        return remote(block, block, rows_send, recv, device)

    def attend_batch(batch, carry):
        for head in range(span // HEAD_DIM):
            lanes = pl.ds(pl.multiple_of(batch * span + head * HEAD_DIM, HEAD_DIM), HEAD_DIM)
            key_head = keys[:, :, lanes].reshape(-1, HEAD_DIM)
            value_head = values[:, :, lanes].reshape(-1, HEAD_DIM)
            scores = lax.dot_general(
                query[:, lanes], key_head, (((1,), (1,)), ((), ())),
                preferred_element_type=jnp.float32,
            )
            scores = scores * (1.0 / math.sqrt(HEAD_DIM)) + bias[...]
            exponent = jnp.exp(scores - jnp.max(scores, axis=-1, keepdims=True))
            totals = jnp.sum(exponent, axis=-1, keepdims=True)
            mixing = (exponent * (1.0 / totals)).astype(jnp.bfloat16)
            mixture = jnp.dot(mixing, value_head, preferred_element_type=jnp.float32)
            rows[batch, place, :, head * HEAD_DIM:(head + 1) * HEAD_DIM] = mixture.astype(jnp.bfloat16)
        rows_copy(batch, place, rows_recv.at[batch], to_across).start()
        rows_copy(batch, place, pair_recv.at[0], to_beside).start()

        mate_step(batch - MATE_LAG)
        relay_step(batch - RELAY_LAG)
        forward_steps(batch)
        return carry

    def relay_step(batch):
        @pl.when(within(batch, batches))
        def _():
            rows_copy(batch, across, rows_recv.at[batch], to_across).wait_recv()
            rows_copy(batch, across, pair_recv.at[1], to_beside).start()

    def forward_round(step, carry):
        mate_step(step - MATE_LAG)
        relay_step(step - RELAY_LAG)
        forward_steps(step)
        return carry

    lax.fori_loop(0, batches, attend_batch, 0)
    gate_copy.start()
    lax.fori_loop(batches, PROJECT_LAG, forward_round, 0)

    def cols_copy(index, slot, device):
        return remote(finished.at[index, slot], out_ref.at[:, columns(index)],
                      cols_send, cols_recv.at[place], device)

    def product(index, receiver, holder):
        whole = weight[index].reshape(owners * depth, PIECE)
        total = None
        for batch in range(batches):
            part = jnp.dot(rows[batch, receiver], whole[batch * span:(batch + 1) * span],
                           preferred_element_type=jnp.float32)
            total = part if total is None else total + part
        return (total * gates[holder, :, columns(index)][0:1]).astype(jnp.bfloat16)

    def receive_place(index):
        out_ref[:, columns(index)] = product(index, place, group)

    def serve(index, slot):
        receiver, holder, device = ((across, 1 - group, to_across), (corner, 1 - group, to_corner), (beside, group, to_beside))[slot]
        finished[index, slot] = product(index, receiver, holder)
        cols_copy(index, slot, device).start()

    def project(step, carry):
        index = step - PROJECT_LAG
        mate_step(step - MATE_LAG)
        relay_step(step - RELAY_LAG)

        @pl.when(index == 0)
        def _():
            gate_copy.wait_recv()
            for at, origin in enumerate((beside, corner)):
                every = rows.at[:, origin]
                remote(every, every, rows_send, pair_recv.at[at], to_beside).wait_recv()
            mine = weight.at[:, owner]
            pltpu.make_async_copy(mine, mine, own_weight).wait()

        @pl.when(jnp.logical_not(balanced(index)))
        def _():
            near_wait(index)

        if lines > 1:
            others = weight.at[index, pl.ds(0, lines - 1)]
            remote(others, others, side_send, far_recv.at[index], to_side).wait_recv()
        serve(index, 0)
        forward_steps(step, 1)
        serve(index, 1)
        forward_steps(step, 0, 1)
        serve(index, 2)

        @pl.when(index > 0)
        def _():
            receive_place(index - 1)

        return carry

    lax.fori_loop(PROJECT_LAG, PROJECT_LAG + pieces, project, 0)
    receive_place(pieces - 1)

    def sent(blocks, send):
        remote(blocks, blocks, send, near_recv.at[0], to_side).wait_send()

    if paired:
        sent(weight.at[pl.ds(0, pieces // 2), pl.ds(0, owners - 1)], side_send)
        sent(weight.at[pl.ds(0, pieces // 2), 0], mate_send)
    else:
        sent(weight.at[:, pl.ds(0, lines)], side_send)
    for at in range(lines):
        if at + 1 < lines:
            @pl.when(line == at)
            def _():
                sent(weight.at[:, pl.ds(0, at + 1)], up_send)
        if at > 0:
            @pl.when(line == at)
            def _():
                sent(weight.at[:, pl.ds(0, lines - at)], down_send)
    for halo in halos:
        halo.wait_send()
    gate_copy.wait_send()
    sent(rows.at[:, pl.ds(0, 3)], rows_send)
    sent(finished, cols_send)

    def quarter_of(origin):
        return out_ref.at[:, pl.ds(pl.multiple_of(origin * quarter, PIECE), quarter)]

    for origin in (beside, across, corner):
        remote(quarter_of(origin), quarter_of(origin), cols_send, cols_recv.at[origin], to_across).wait_recv()


def fused(queries, key_value, keep, windows, gate, out_weight):
    frames, spots, features = queries.shape[1:]
    model_width = gate.shape[1]
    owners = lax.axis_size("owner")
    tokens = frames * spots
    depth = out_weight.shape[0]
    pieces = model_width // 4 // PIECE
    span = HEAD_GROUP * HEAD_DIM
    batches = features // span
    lines = owners // 2
    bf16 = jnp.bfloat16
    dma = pltpu.SemaphoreType.DMA
    whole = pl.BlockSpec(memory_space=pl.ANY)
    result = pl.pallas_call(
        fused_kernel,
        out_shape=pltpu.VMEM((tokens, model_width), bf16),
        in_specs=[whole] * 6,
        out_specs=pl.BlockSpec(memory_space=pltpu.VMEM),
        scratch_shapes=[
            pltpu.SMEM(keep.shape, jnp.int32),
            pltpu.SMEM(windows.shape, jnp.int32),
            pltpu.VMEM((tokens, features), bf16),
            pltpu.VMEM((frames + HALO, spots, features), bf16),
            pltpu.VMEM((frames + HALO, spots, features), bf16),
            pltpu.VMEM((pieces, owners, depth, PIECE), bf16),
            pltpu.VMEM((batches, 4, tokens, span), bf16),
            pltpu.VMEM((pieces, 3, tokens, PIECE), bf16),
            pltpu.VMEM((2, 8, model_width), jnp.float32),
            pltpu.VMEM(gate.shape, jnp.float32),
            pltpu.VMEM((tokens, tokens + spots), jnp.float32),
            dma((6,)), dma((2,)), dma((2,)), dma, dma, dma,
            dma((pieces, max(lines - 1, 1))), dma((pieces,)), dma((pieces,)), dma, dma, dma, dma,
            dma((batches,)), dma((2,)), dma,
            dma((4,)), dma,
        ],
        compiler_params=pltpu.CompilerParams(
            collective_id=0, has_side_effects=True, vmem_limit_bytes=56 * 2**20,
        ),
    )(
        queries.reshape(tokens, features), key_value.reshape(2, frames, spots, features),
        out_weight, gate, keep, windows,
    )
    return result.reshape(1, frames, spots, model_width)


def on_device(queries, key_value, keep, windows, gate, out_weight):
    frames, spots, features = queries.shape[1:]
    fits = (
        lax.axis_size("slab") == 2
        and lax.axis_size("groups") == 2
        and lax.axis_size("owner") % 2 == 0
        and out_weight.shape[0] % 16 == 0
        and spots % 16 == 0
        and spots % WB == 0
        and features % (HEAD_GROUP * HEAD_DIM) == 0
        and gate.shape[1] % (8 * PIECE) == 0
    )
    chosen = fused if fits else plain
    return chosen(queries, key_value, keep, windows, gate, out_weight)


def solution(mesh):
    placed = (
        P(("groups", "owner"), "slab", None, None),
        P(None, ("groups", "owner"), "slab", None, None),
        P("groups"),
        P("groups", None),
        P("groups", None),
        P("owner", None),
    )
    return jax.shard_map(
        on_device,
        mesh=mesh,
        in_specs=placed,
        out_specs=P(("groups", "owner"), "slab", None, None),
        check_vma=False,
    )
```
